32 devices in a mesh: groups: 2 (over y), vox: 4 (over z), freq: 2 (over x), sub: 2 (over core).
Axes of the slice: x: 2, y: 2, z: 4, core: 2. Of those that a mesh axis runs over, the one named last changes fastest.
Arguments:
- residual: bfloat16 [4, 1024, 1024], P(('groups', 'freq'), 'vox', 'sub'), parts along dimension 0, may hold values from -6 to 6
- green: bfloat16 [4, 1024, 8192], P(('groups', 'freq'), None, 'vox'), parts along dimension 0, may hold values from -0.15625 to 0.15625
- active: int32 [4, 1024], P(('groups', 'freq')), parts along dimension 0, may hold values 0 or 1
- aperture: int32 [4], P(('groups', 'freq')), parts along dimension 0, may hold values from 256 to 511
- step_gain: float32 [4], P(('groups', 'freq')), parts along dimension 0, may hold values from 6 to 24
- block_region: int32 [128], P(('groups', 'vox')), parts along dimension 0, may hold values from 0 to 15
- strength: float32 [16], replicated, may hold values from 0.1 to 1
Outputs:
- updated: float32 [4, 1024, 1024], P(('groups', 'freq'), 'vox', 'sub'), parts along dimension 0
The draws below stay inside these ranges and needn't reach their ends.
There are 2 independent parts, one for each index of `groups`. The reference program is written for one: setup_inputs(seed, part) draws one part's arguments, and reference() takes and returns one part's arrays. A program takes and returns all parts, laid end to end along the dimension named above; an argument that names none is the same for every part. Nothing has to cross between parts.
All inputs are finite; a program needn't handle non-finite values. No bound on the sum of `active` on one device may be relied on, other than what follows from the above.
Results may differ from the reference program's by a relative error of at most 0.0026.
Values may be sent and summed in bfloat16 or wider, within the bound.
A program may use at most 64 MiB of HBM per device.

```python
import math
import jax
import jax.numpy as jnp
from jax import lax

NE = 1024
BLOCK = 128
REGIONS = 16
FREQS = 2
VOXELS = 8192
NBLK = 64


def place_ends(result, own_key, low, high):
    longest = result.shape.index(max(result.shape))
    spots = []
    for shift in (0, 1):
        where = [jax.random.randint(jax.random.fold_in(own_key, axis), (), 0, length) for axis, length in enumerate(result.shape)]
        where[longest] = (where[longest] + shift) % result.shape[longest]
        spots.append(tuple(where))
    return result.at[spots[0]].set(low).at[spots[1]].set(high)


def strengthened(values, rng, source, target, shards_of, factor):
    def block_of(position):
        return (jnp.arange(values.shape[position]) // (values.shape[position] // shards_of)).reshape((-1,) + (1,) * (values.ndim - 1 - position))

    one_side = jax.random.permutation(rng, shards_of)[block_of(target)]
    other_side = (block_of(target) + shards_of // 2) % shards_of
    return jnp.where((block_of(source) == one_side) | (block_of(source) == other_side), factor * values, values)


def block_levels(own_key, shape, pieces, low, largest):
    def one(dim, blocks):
        steps = jax.random.uniform(jax.random.fold_in(jax.random.fold_in(own_key, 6), dim), (blocks,), jnp.float32, low / len(pieces), largest / len(pieces))
        return jnp.repeat(jnp.exp(steps), shape[dim] // blocks).reshape((-1,) + (1,) * (len(shape) - dim - 1))

    loudness = one(*pieces[0])
    for cut in pieces[1:]:
        loudness = loudness * one(*cut)
    return loudness


def normal_values(key, extent, width, bound, split=(), kind=jnp.bfloat16):
    drawn = jax.random.normal(key, extent, jnp.float32) * width
    if len(split) > 0:
        drawn = block_levels(key, extent, split, -0.22, 0.18) * drawn
    return jnp.clip(drawn, min=-bound, max=bound).astype(kind)


def heavy_noise(stream_key, extent, scale, most, cuts, heavy, kind=jnp.bfloat16):
    array = scale * jax.random.normal(stream_key, extent, jnp.float32)
    if cuts:
        array = array * block_levels(stream_key, extent, cuts, -0.22, 0.18)
    return jnp.clip(strengthened(array, jax.random.fold_in(stream_key, 3), *heavy), -most, most).astype(kind)


def setup_inputs(seed: int = 0, part: int = 0) -> dict:
    arg_keys = jax.random.split(jax.random.key(seed), 8)
    own_keys = jax.random.split(jax.random.fold_in(arg_keys[7], part), 8)
    return {
        "residual": normal_values(own_keys[0], (FREQS, NE, NE), 1.0, 6.0, ((0, 2), (1, 4), (2, 2))),
        "green": heavy_noise(own_keys[1], (FREQS, NE, VOXELS), (3 * NE) ** -0.5, 0.15625, ((0, 2), (2, 4)), (2, 1, 4, 2.0)),
        "active": place_ends((jax.random.randint(own_keys[2], (FREQS, NE), 0, 8) < 7).astype(jnp.int32), jax.random.fold_in(own_keys[2], 1), 0, 1),
        "aperture": jax.random.randint(own_keys[3], (FREQS,), NE // 4, NE // 2).astype(jnp.int32),
        "step_gain": jnp.clip(jnp.exp(math.log(24.0) - 1.3862944 * jax.random.uniform(own_keys[4], (FREQS,), jnp.float32) ** block_levels(own_keys[4], (FREQS,), ((0, 2),), -0.2, 0.2)), 6.0, 24.0),
        "block_region": place_ends(jax.random.randint(own_keys[5], (NBLK,), 0, REGIONS), jax.random.fold_in(own_keys[5], 1), 0, REGIONS - 1).astype(jnp.int32),
        "strength": jnp.clip(jnp.exp(jax.random.uniform(arg_keys[6], (REGIONS,), jnp.float32, math.log(0.1), math.log(1.0))), 0.1, 1.0),
    }


smooth_sq = 0.0625

def build_mask(active, aperture):
    element_ids = jnp.arange(NE, dtype=jnp.int32)
    distance = jnp.abs(element_ids[:, None] - element_ids[None, :])
    in_band = (distance[None, :, :] <= aperture[:, None, None]).astype(jnp.int32)
    return active[:, :, None] * active[:, None, :] * in_band

def penalize(image_sum, strength_map):
    return image_sum - strength_map * image_sum / jnp.sqrt(image_sum * image_sum + smooth_sq)

def reference(residual, green, active, aperture, step_gain, block_region, strength):
    pair_mask = build_mask(active, aperture)
    masked = residual * pair_mask.astype(jnp.bfloat16)

    def image_one(operands):
        masked_f, green_f = operands
        beamed = jnp.dot(masked_f.T, green_f, preferred_element_type=jnp.float32)
        return lax.optimization_barrier(jnp.sum(green_f.astype(jnp.float32) * beamed, axis=0))
    image_sum = lax.optimization_barrier(jnp.sum(lax.map(image_one, (masked, green)), axis=0))
    strength_map = jnp.repeat(strength[block_region], BLOCK)
    scaled = penalize(image_sum, strength_map)

    def gradient_one(green_f):
        weighted = (green_f.astype(jnp.float32) * scaled[None, :]).astype(jnp.bfloat16)
        return jnp.dot(green_f, weighted.T, preferred_element_type=jnp.float32)
    gradient = lax.map(gradient_one, green)
    return pair_mask.astype(jnp.float32) * (residual.astype(jnp.float32) - step_gain[:, None, None] * gradient)
```

```python
import jax
import jax.numpy as jnp
from jax import lax
from jax.experimental import pallas as pl
from jax.experimental.pallas import tpu as pltpu
from jax.sharding import PartitionSpec as P

BLOCK = 128
LANES = 128
APERTURE_MAX = 511
smooth_sq = 0.0625
FULL, UP, DOWN = range(3)
MESH = pl.DeviceIdType.MESH


def penalize(image_sum, strength_map):
    return image_sum - strength_map * image_sum / jnp.sqrt(image_sum * image_sum + smooth_sq)


def make_kernel(n, nf, ns, rows, cols, ne, vox_local, n_blocks, regions):
    tile = min(rows, LANES)
    per = rows // tile
    col_tiles = cols // LANES
    vchunk = min(512, vox_local)
    peers = nf * ns

    def kernel(
        res, green, active_in, aperture_in, gain_in, region_in, strength_in, out,
        active, aperture, gain, region, strength, sem_small,
        allm, gv, act_col, mm, img, ar_send, ar_land, wgt, gacc, flipped, send_buf, land_r, land_l,
        sem_g, sem_own, agr_s, agr_r, agl_s, agl_r, ar_s, ar_r, rsr_s, rsr_r, rsl_s, rsl_r,
    ):
        z = lax.axis_index("vox")
        f = lax.axis_index("freq")
        s = lax.axis_index("sub")
        has_up = z < n - 1
        has_down = z > 0
        up = {"vox": jnp.minimum(z + 1, n - 1)}
        down = {"vox": jnp.maximum(z - 1, 0)}

        def row_of(block):
            return pl.multiple_of(block * rows, rows)

        small = [
            pltpu.make_async_copy(a, b, sem_small.at[i])
            for i, (a, b) in enumerate((
                (active_in, active), (aperture_in, aperture), (gain_in, gain),
                (region_in, region), (strength_in, strength),
            ))
        ]
        for c in small:
            c.start()
        own_copy = pltpu.make_async_copy(res, allm.at[pl.ds(row_of(z), rows), :], sem_own)
        own_copy.start()
        green_copy = pltpu.make_async_copy(green, gv, sem_g)
        green_copy.start()

        def peer(k):
            df, ds = k // ns, k % ns
            return {"freq": lax.rem(f + df, nf), "sub": lax.rem(s + ds, ns)}

        barrier = pltpu.get_barrier_semaphore()
        for k in range(1, peers):
            pl.semaphore_signal(barrier, inc=1, device_id=peer(k), device_id_type=MESH)

        @pl.when(has_up)
        def _():
            pl.semaphore_signal(barrier, inc=1, device_id=up, device_id_type=MESH)

        @pl.when(has_down)
        def _():
            pl.semaphore_signal(barrier, inc=1, device_id=down, device_id_type=MESH)

        pl.semaphore_wait(barrier, peers - 1 + has_up.astype(jnp.int32) + has_down.astype(jnp.int32))

        def square(q):
            local = q * tile - s * cols
            inside = (local >= 0) & (local < cols)
            return inside, lax.div(jnp.clip(local, 0, cols - 1), LANES)

        def band(q, kind):
            reach = q * tile - s * cols + ne
            shift = ne // LANES + APERTURE_MAX // LANES + 1
            lift = LANES * (shift - ne // LANES)
            first = lax.div(reach + lift - APERTURE_MAX, LANES) - shift
            last = lax.div(reach + lift + tile - 1 + APERTURE_MAX, LANES) - shift + 1
            first = jnp.clip(first, 0, col_tiles)
            last = jnp.clip(last, 0, col_tiles)
            if kind != FULL:
                inside, diag = square(q)
            if kind == UP:
                last = jnp.where(inside, jnp.minimum(last, diag + 1), last)
            if kind == DOWN:
                first = jnp.where(inside, jnp.maximum(first, diag), first)
            return first, last - first

        def per_width(q, fn, kind=FULL):
            first, count = band(q, kind)
            for w in range(1, col_tiles + 1):
                @pl.when(count == w)
                def _(w=w):
                    fn(pl.ds(pl.multiple_of(first * LANES, LANES), w * LANES))

        def tile_rows(q):
            return pl.ds(pl.multiple_of(q * tile, tile), tile)

        def remote(src, dst, send, recv, target):
            return pltpu.make_async_remote_copy(
                src_ref=src, dst_ref=dst, send_sem=send, recv_sem=recv,
                device_id=target, device_id_type=MESH,
            )

        def each_tile(block, make, act, kind=FULL):
            for t in range(per):
                q = block * per + t
                per_width(q, lambda c, q=q: act(make(q, c)), kind)

        def gather_up(q, c):
            a = allm.at[tile_rows(q), c]
            return remote(a, a, agr_s.at[q], agr_r.at[q], up)

        def gather_down(q, c):
            a = allm.at[tile_rows(q), c]
            return remote(a, a, agl_s.at[q], agl_r.at[q], down)

        for t in range(per):
            q = z * per + t

            def first_up(c, q=q, t=t):
                remote(res.at[pl.ds(t * tile, tile), c], allm.at[tile_rows(q), c],
                       agr_s.at[q], agr_r.at[q], up).start()

            def first_down(c, q=q, t=t):
                remote(res.at[pl.ds(t * tile, tile), c], allm.at[tile_rows(q), c],
                       agl_s.at[q], agl_r.at[q], down).start()

            @pl.when(has_up)
            def _():
                per_width(q, first_up)

            @pl.when(has_down)
            def _():
                per_width(q, first_down)

        for c in small:
            c.wait()
        for i in range(ne // LANES):
            line = active[0:1, i * LANES:(i + 1) * LANES].astype(jnp.float32)
            act_col[i * LANES:(i + 1) * LANES, :] = jnp.broadcast_to(line, (LANES, LANES)).T
        img[...] = jnp.zeros_like(img)
        col0 = pl.multiple_of(s * cols, cols)

        def pair_mask(block):
            r0 = row_of(block)
            rr = lax.broadcasted_iota(jnp.int32, (rows, cols), 0) + r0
            cc = lax.broadcasted_iota(jnp.int32, (rows, cols), 1) + col0
            in_band = jnp.abs(rr - cc) <= aperture[0]
            row_on = act_col[pl.ds(r0, rows), 0:1] > 0.5
            col_on = active[0:1, pl.ds(col0, cols)] > 0
            return in_band & row_on & col_on

        def image_part(block):
            r0 = row_of(block)
            value = allm[pl.ds(r0, rows), :].astype(jnp.float32)
            mm[...] = jnp.where(pair_mask(block), value, 0.0).astype(jnp.bfloat16)

            @pl.loop(0, vox_local // vchunk)
            def _(v):
                vs = pl.ds(pl.multiple_of(v * vchunk, vchunk), vchunk)
                y = jnp.dot(mm[...], gv[pl.ds(col0, cols), vs], preferred_element_type=jnp.float32)
                y = y * gv[pl.ds(r0, rows), vs].astype(jnp.float32)
                img[:, vs] += jnp.sum(y.reshape(rows // 8, 8, vchunk), axis=0)

        own_copy.wait()
        green_copy.wait()
        image_part(z)

        @pl.loop(0, n - 1)
        def _(step):
            from_below = z - 1 - step
            from_above = z + 1 + step
            for t in range(per):
                @pl.when(from_below >= 0)
                def _():
                    q = from_below * per + t

                    def land(c):
                        gather_up(q, c).wait_recv()

                        @pl.when(has_up)
                        def _():
                            gather_up(q, c).start()
                    per_width(q, land)

                @pl.when(from_above < n)
                def _():
                    q = from_above * per + t

                    def land(c):
                        gather_down(q, c).wait_recv()

                        @pl.when(has_down)
                        def _():
                            gather_down(q, c).start()
                    per_width(q, land)

            @pl.when(from_below >= 0)
            def _():
                image_part(from_below)

            @pl.when(from_above < n)
            def _():
                image_part(from_above)

        ar_send[...] = jnp.sum(img[...], axis=0, keepdims=True)
        exchanges = [
            remote(ar_send, ar_land.at[k], ar_s.at[k], ar_r.at[k], peer(k)) for k in range(1, peers)
        ]
        for e in exchanges:
            e.start()
        strength_map = jnp.concatenate(
            [jnp.full((1, BLOCK), strength[region[b]], jnp.float32) for b in range(n_blocks)], axis=1
        )

        @pl.loop(0, n)
        def _(b):
            @pl.when(has_up & (b <= z))
            def _():
                each_tile(b, gather_up, lambda c: c.wait_send())

            @pl.when(has_down & (b >= z))
            def _():
                each_tile(b, gather_down, lambda c: c.wait_send())

        for e in exchanges:
            e.wait_recv()
        total = ar_send[...]
        for k in range(1, peers):
            total = total + ar_land[k]
        img[0:1, :] = penalize(total, strength_map)

        wrows = 32

        @pl.loop(0, cols // wrows)
        def _(i):
            src = pl.ds(pl.multiple_of(col0 + i * wrows, wrows), wrows)
            dst = pl.ds(pl.multiple_of(i * wrows, wrows), wrows)
            wgt[dst, :] = (gv[src, :].astype(jnp.float32) * img[0:1, :]).astype(jnp.bfloat16)

        def scatter_up(q, c):
            return remote(send_buf.at[tile_rows(q), c], land_r.at[tile_rows(q), c],
                          rsr_s.at[q], rsr_r.at[q], up)

        def scatter_down(q, c):
            return remote(send_buf.at[tile_rows(q), c], land_l.at[tile_rows(q), c],
                          rsl_s.at[q], rsl_r.at[q], down)

        def partial_step(k, ends):
            lo, hi = ends
            use_hi = (hi > z) & ((lo >= z) | (z + (n - 1 - hi) <= (n - 1 - z) + lo))
            d = jnp.where(use_hi, hi, lo)
            rs = pl.ds(row_of(d), rows)
            part = lax.dot_general(
                gv[rs, :], wgt[...], (((1,), (1,)), ((), ())), preferred_element_type=jnp.float32
            )
            gacc[rs, :] = part
            sends_up = (d > z) & jnp.logical_not(has_down)
            sends_down = (d < z) & jnp.logical_not(has_up)

            @pl.when(sends_up | sends_down)
            def _():
                send_buf[rs, :] = part.astype(jnp.bfloat16)

            @pl.when(sends_up)
            def _():
                each_tile(d, scatter_up, lambda c: c.start(), UP)

            @pl.when(sends_down)
            def _():
                each_tile(d, scatter_down, lambda c: c.start(), DOWN)

            step_hi = use_hi.astype(jnp.int32)
            return lo + 1 - step_hi, hi - step_hi

        lax.fori_loop(0, n, partial_step, (jnp.int32(0), jnp.int32(n - 1)))

        @pl.loop(0, n - 1)
        def _(slot):
            @pl.when(has_down & (slot >= z))
            def _():
                d = z + n - 1 - slot
                for t in range(per):
                    q = d * per + t

                    def add(c):
                        scatter_up(q, c).wait_recv()
                        send_buf[tile_rows(q), c] = (
                            gacc[tile_rows(q), c] + land_r[tile_rows(q), c].astype(jnp.float32)
                        ).astype(jnp.bfloat16)
                        scatter_up(q, c).start()
                    per_width(q, add, UP)

            @pl.when(has_up & (slot >= n - 1 - z))
            def _():
                d = slot - (n - 1 - z)
                for t in range(per):
                    q = d * per + t

                    def add(c):
                        scatter_down(q, c).wait_recv()
                        send_buf[tile_rows(q), c] = (
                            gacc[tile_rows(q), c] + land_l[tile_rows(q), c].astype(jnp.float32)
                        ).astype(jnp.bfloat16)
                        scatter_down(q, c).start()
                    per_width(q, add, DOWN)

        @pl.when(has_down)
        def _():
            each_tile(z, scatter_up, lambda c: c.wait_recv(), UP)

        @pl.when(has_up)
        def _():
            each_tile(z, scatter_down, lambda c: c.wait_recv(), DOWN)

        mine = pl.ds(row_of(z), rows)
        def add_landed(land, there, q, mirrored):
            inside, diag = square(q)
            offset = lax.rem(q * tile, LANES)
            for j in range(col_tiles):
                c = slice(j * LANES, (j + 1) * LANES)
                flip = inside & mirrored(j, diag)

                @pl.when(there & jnp.logical_not(flip))
                def _():
                    gacc[tile_rows(q), c] += land[tile_rows(q), c].astype(jnp.float32)

                @pl.when(there & flip)
                def _():
                    twin = pl.ds(pl.multiple_of(col0 + j * LANES, LANES), LANES)
                    own = pl.ds(pl.multiple_of(diag * LANES, LANES), LANES)
                    flipped[...] = land[twin, own].astype(jnp.float32).T
                    gacc[tile_rows(q), c] += flipped[pl.ds(pl.multiple_of(offset, tile), tile), :]

        for t in range(per):
            add_landed(land_r, has_down, z * per + t, lambda j, diag: j > diag)
            add_landed(land_l, has_up, z * per + t, lambda j, diag: j < diag)
        gradient = gacc[mine, :]
        data = allm[mine, :].astype(jnp.float32)
        out[...] = jnp.where(pair_mask(z), data - gain[0] * gradient, 0.0)

        for e in exchanges:
            e.wait_send()

        @pl.loop(0, n)
        def _(b):
            @pl.when(has_up & (b > z))
            def _():
                each_tile(b, scatter_up, lambda c: c.wait_send(), UP)

            @pl.when(has_down & (b < z))
            def _():
                each_tile(b, scatter_down, lambda c: c.wait_send(), DOWN)

    tiles = n * per
    dma = pltpu.SemaphoreType.DMA
    scratch = [
        pltpu.VMEM((1, ne), jnp.int32),
        pltpu.SMEM((1,), jnp.int32),
        pltpu.SMEM((1,), jnp.float32),
        pltpu.SMEM((n_blocks,), jnp.int32),
        pltpu.SMEM((regions,), jnp.float32),
        dma((5,)),
        pltpu.VMEM((ne, cols), jnp.bfloat16),
        pltpu.VMEM((ne, vox_local), jnp.bfloat16),
        pltpu.VMEM((ne, LANES), jnp.float32),
        pltpu.VMEM((rows, cols), jnp.bfloat16),
        pltpu.VMEM((8, vox_local), jnp.float32),
        pltpu.VMEM((1, vox_local), jnp.float32),
        pltpu.VMEM((peers, 1, vox_local), jnp.float32),
        pltpu.VMEM((cols, vox_local), jnp.bfloat16),
        pltpu.VMEM((ne, cols), jnp.float32),
        pltpu.VMEM((LANES, LANES), jnp.float32),
        pltpu.VMEM((ne, cols), jnp.bfloat16),
        pltpu.VMEM((ne, cols), jnp.bfloat16),
        pltpu.VMEM((ne, cols), jnp.bfloat16),
        dma, dma,
        dma((tiles,)), dma((tiles,)), dma((tiles,)), dma((tiles,)),
        dma((peers,)), dma((peers,)),
        dma((tiles,)), dma((tiles,)), dma((tiles,)), dma((tiles,)),
    ]
    return kernel, scratch


def solution(mesh):
    sizes = dict(mesh.shape)

    def body(residual, green, active, aperture, step_gain, block_region, strength):
        _, rows, cols = residual.shape
        _, ne, vox_local = green.shape
        kernel, scratch = make_kernel(
            sizes["vox"], sizes["freq"], sizes["sub"], rows, cols, ne, vox_local,
            block_region.shape[0], strength.shape[0],
        )
        vmem = pl.BlockSpec(memory_space=pltpu.VMEM)
        hbm = pl.BlockSpec(memory_space=pltpu.HBM)
        updated = pl.pallas_call(
            kernel,
            out_shape=jax.ShapeDtypeStruct((rows, cols), jnp.float32),
            in_specs=[hbm] * 7,
            out_specs=vmem,
            scratch_shapes=scratch,
            compiler_params=pltpu.CompilerParams(
                collective_id=0, has_side_effects=True, vmem_limit_bytes=24 * 1024 * 1024
            ),
            name="imaging_step",
        )(*[
            pltpu.with_memory_space_constraint(a, pltpu.HBM) if a.size > 1 else a
            for a in (residual[0], green[0], active, aperture, step_gain, block_region, strength)
        ])
        return updated[None]

    in_specs = (
        P(("groups", "freq"), "vox", "sub"),
        P(("groups", "freq"), None, "vox"),
        P(("groups", "freq"), None),
        P(("groups", "freq")),
        P(("groups", "freq")),
        P(("groups", "vox")),
        P(),
    )
    out_specs = P(("groups", "freq"), "vox", "sub")
    return jax.shard_map(body, mesh=mesh, in_specs=in_specs, out_specs=out_specs, check_vma=False)
```

```python
import heapq
import itertools

import jax
import jax.numpy as jnp
from jax import lax
from jax.experimental import pallas as pl
from jax.experimental.pallas import tpu as pltpu
from jax.sharding import PartitionSpec as P

BLOCK = 128
LANES = 128
APERTURE_MAX = 511
smooth_sq = 0.0625
FULL, UP, DOWN = range(3)
MESH = pl.DeviceIdType.MESH
REACH = (APERTURE_MAX + LANES - 1) // LANES
CHUNK = 512
LN2 = 0.6931471805599453
STEPS = 32600.0


def penalize(image_sum, strength_map):
    return image_sum - strength_map * image_sum / jnp.sqrt(image_sum * image_sum + smooth_sq)


WIRE, HOP_FIRST, HOP = 0.354, 2.3, 2.0
IMAGE, PLACE, MERGE, PARTIAL, WEIGHT, ADD = 0.47, 0.04, 0.1, 0.47, 0.2, 0.12
EXCHANGE, LAG, PATIENCE, SLACK, ACROSS = 2.8, 0.0, 1.0, 0.8, 1.0


def tile_pairs(tiles, reach):
    return [(p, q) for p in range(tiles) for q in range(p, min(tiles, p + reach + 1))]


def riders(pairs, n, per, half, cores):
    if cores != 2 or half != REACH or REACH % per or REACH * LANES <= APERTURE_MAX:
        return {}
    index = {pair: a for a, pair in enumerate(pairs)}
    return {a: (index[p, p], index[q, q]) for a, (p, q) in enumerate(pairs) if q - p == REACH}


def lanes_of(pairs, n, per, half, cores, ride):
    sizes = {}
    for p, q in pairs:
        sizes[p // per, q // per] = sizes.get((p // per, q // per), 0) + 1
    lanes = {}
    for k in range(n):
        load, follows, light = [0] * cores, {}, {}
        for a in ride:
            i, j = pairs[a][0] // per, pairs[a][1] // per
            for own, there in ((i, k > i), (j, k < j)):
                if there:
                    follows[own, own] = i, j
                    light[own, own] = light.get((own, own), 0) + 1

        def rank(block, k=k):
            i, j = block
            far = n - 1 - j if k == 0 else i if k == n - 1 else k not in block
            return far, k not in block, -sizes[block], block

        def weight(block, k=k, light=light):
            return (sizes[block] - light.get(block, 0)) * (block != (k, k) or 0 < k < n - 1)

        order = sorted(sizes, key=rank)
        forced = {(i, j): (j if k == i else i) * per // half for i, j in order if k in (i, j)}
        free = [block for block in order if block not in forced and block not in follows]

        def filled(where, follows=follows, forced=forced):
            return {**{block: where[to] for block, to in follows.items() if block not in forced}, **where}

        def unevenness(picks):
            where = filled({**forced, **dict(zip(free, picks))})
            total, worst = [0] * cores, []
            for at, block in enumerate(order):
                total[where[block]] += weight(block)
                if at + 1 == len(order) or rank(order[at + 1])[0] != rank(block)[0]:
                    worst.append(max(total) - min(total))
            return sum(worst), picks

        if cores ** len(free) <= 4096:
            chosen = dict(zip(free, min(map(unevenness, itertools.product(range(cores), repeat=len(free))))[1]))
        else:
            chosen = {}
            for block in free:
                chosen[block] = load.index(min(load))
                load[chosen[block]] += weight(block)
        chosen = filled({**forced, **chosen})
        for a, (p, q) in enumerate(pairs):
            lanes[a, k] = chosen[p // per, q // per]
    return lanes


def colours(uses):
    taken, chosen = {}, {}
    for a in sorted(uses, key=lambda a: (-len(uses[a]), a)):
        colour = 0
        while any(colour in taken.setdefault(place, set()) for place in uses[a]):
            colour += 1
        for place in uses[a]:
            taken[place].add(colour)
        chosen[a] = colour
    return chosen


class Network:
    def __init__(self, cores, hop):
        self.cores, self.hop, self.queue, self.count = cores, hop, [], 0
        self.wires = {}

    def post(self, time, what):
        self.count += 1
        heapq.heappush(self.queue, (time, self.count, what))

    def send(self, k, c, step, time, what):
        lines, turn, free = self.wires.setdefault((k, step), ([[] for _ in range(self.cores)], 0, 0.0))
        lines[c].append(what)
        self.post(max(time, free), ("wire", k, step, 0, 0))

    def serve(self, k, step, now):
        lines, turn, free = self.wires[k, step]
        if free > now + 1e-9:
            return
        for c in range(self.cores):
            line = lines[(turn + c) % self.cores]
            if line:
                self.post(now + WIRE + self.hop, line.pop(0))
                self.wires[k, step] = lines, (turn + c + 1) % self.cores, now + WIRE
                self.post(now + WIRE, ("wire", k, step, 0, 0))
                return


def gather_plan(pairs, n, per, half, cores, lanes, ride):
    net = Network(cores, HOP_FIRST)
    own, events = {}, {}
    seen, busy, missing = set(), {}, {}
    low = {pair[0]: a for a, pair in ride.items()}
    high = {pair[1]: a for a, pair in ride.items()}
    for p, q in pairs:
        for k in range(n):
            missing[p // per, q // per, k] = missing.get((p // per, q // per, k), 0) + 1

    def send(k, c, a, step, kind, now):
        net.send(k, c, step, now, (kind, k + step, lanes[a, k + step], a, 0))

    for k in range(n):
        for c in range(cores):
            own[k, c], events[k, c] = [], []
        mine = []
        for a, (p, q) in enumerate(pairs):
            i, j = p // per, q // per
            c = lanes[a, k]
            if i == k < j:
                mine.append((j - i, c, a, 0, q, 1, 0))
            elif i < k == j:
                mine.append((j - i, c, a, 1, p, 0, 1))
            elif i == j == k:
                mine.append((n, c, a, 0, q, int(p == q and a not in low), int(p == q and a not in high)))
                if p < q:
                    mine.append((n, c, a, 1, p, 0, 0))
        for _, c, a, second, other, up, down in sorted(mine):
            p, q = pairs[a]
            up, down = up and k < n - 1 and a not in ride, down and k > 0 and a not in ride
            side = a in low and k < n - 1 or a in high and k > 0
            own[k, c].append((a, second, (q if second else p) % per, other % half, up, down, side))
            if side:
                net.post(0.1 + WIRE + ACROSS, ("lift", k, 1 - c, a, 0))
            if up:
                send(k, c, a, 1, "A", 0.1)
            if down:
                send(k, c, a, -1, "B" if second else "A", 0.1)
        for c in range(cores):
            here = [a for a, (p, q) in enumerate(pairs) if p // per == q // per == k and lanes[a, k] == c]
            for a in sorted(here, key=lambda a: pairs[a][0] == pairs[a][1]):
                net.post(0.5, ("own", k, c, a, 0))
    while net.queue:
        now, _, (kind, k, c, a, _) = heapq.heappop(net.queue)
        if kind == "wire":
            net.serve(k, c, now)
            continue
        at = busy.get((k, c), 0.0)
        if at > now + 1e-9:
            net.post(at, (kind, k, c, a, 0))
            continue
        p, q = pairs[a]
        i, j = p // per, q // per
        e = dict(a=a, wait=int(kind != "own"), second=int(kind == "B"), fup=0, fdn=0, merge=0, cup=0, cdn=0, comp=0, run=0)
        e.update(blend=0, ride=0, lift=0, other=0, lower=0, rest=0)
        if kind == "lift":
            up = a in low
            e.update(a=low[a] if up else high[a], second=int(not up), fup=int(up), fdn=int(not up))
            e.update(lift=1, blend=1, other=a, lower=int(not up))
            a = e["a"]
        elif kind in ("rideA", "rideB"):
            e.update(wait=0, ride=1, comp=1, lower=int(kind == "rideB"), other=low[a] if k > i else high[a])
        elif kind == "own":
            e["comp"] = 1
            if p < q:
                e.update(merge=1, cup=int(k < n - 1), cdn=int(k > 0))
        elif j < k:
            e.update(fup=int(k < n - 1), comp=1)
        elif i > k:
            e.update(fdn=int(k > 0), comp=1)
        else:
            if kind == "A":
                e["fup"] = int(k < j)
            else:
                e["fdn"] = int(k > i)
            whole = k in (i, j) or (a, k) in seen
            seen.add((a, k))
            if whole:
                e.update(merge=1, comp=1, cup=int(k == j and k < n - 1), cdn=int(k == i and k > 0))
                e.update(blend=int(a in ride and k in (i, j)), lower=int(k == i))
        if a in ride and kind in ("A", "B"):
            if kind == "A" and k > i:
                net.post(now, ("rideA", k, c, ride[a][0], 0))
            if k < j and (kind == "B" or k < i):
                net.post(now, ("rideB" if kind == "B" else "rideA", k, c, ride[a][1], 0))
        for flag, step, sent in (("fup", 1, "A"), ("fdn", -1, "B" if e["second"] else "A"), ("cup", 1, "A"), ("cdn", -1, "A")):
            if e[flag]:
                send(k, c, a, step, sent, now + 0.05 + MERGE * e["merge"])
        if e["comp"]:
            block = pairs[a][0] // per, pairs[a][1] // per, k
            missing[block] -= 1
            e["run"] = int(missing[block] == 0)
            e["rest"] = int(e["run"] and block[0] <= k <= block[1])
        busy[k, c] = now + 0.06 + MERGE * (e["merge"] + e["ride"] + e["blend"] * (1 - e["merge"])) + PLACE * e["comp"] + IMAGE * e["run"]
        events[k, c].append(e)
    return own, events, [max(busy[k, c] for c in range(cores)) for k in range(n)]


def scatter_plan(pairs, n, per, half, cores, lanes, ride, starts):
    low = {pair[0]: a for a, pair in ride.items()}
    high = {pair[1]: a for a, pair in ride.items()}

    def ends(a):
        return pairs[a][0] // per, pairs[a][1] // per

    def run(order):
        net = Network(cores, HOP)
        events = {key: [] for key in order}
        busy, got, weighted, ready = {}, {}, set(), set()
        made = {key: 0 for key in order}
        waiting = {key: [] for key in order}
        for k, c in order:
            busy[k, c] = starts[k]
            net.post(starts[k], ("go", k, c, -1, 0))

        def handle(k, c, a, kind, now):
            i, j = ends(a)
            e = dict(a=a, comp=int(kind == "D"), first=0, wait=int(kind in ("U", "V")), v=int(kind in ("V", "down")))
            e.update(u=int(kind == "U"), up=0, dn=0, fini=0, finj=0, blend=0, side=0, other=0, mean=0, second=0)
            cost = ADD
            if kind == "D":
                e["first"] = int((j, k, c) not in weighted)
                weighted.add((j, k, c))
                e["mean"] = int(made[k, c] > 1 or 0 < k < n - 1)
                if e["mean"]:
                    e["second"] = int((i, k, c) not in weighted)
                    weighted.add((i, k, c))
                cost = PARTIAL * (1 + e["mean"]) + WEIGHT * (e["first"] + e["second"]) + 0.06
            elif not e["wait"]:
                e["up"], e["dn"] = int(kind == "up"), int(kind == "down")
            else:
                got.setdefault((a, k), set()).add(kind)
                e["up"], e["dn"] = int(kind == "U" and k < j), int(kind == "V" and k > i)
                need = int(0 < k <= j) + int(i <= k < n - 1)
                if k in (i, j) and len(got[a, k]) == need:
                    e.update(fini=int(k == i), finj=int(k == j and pairs[a][0] < pairs[a][1]))
            if a in ride:
                e["blend"] = int(e["up"] or e["dn"])
                if e["wait"] and k == (j if kind == "U" else i):
                    d = ride[a][kind == "U"]
                    e.update(side=1, other=d)
                    cost += 0.1
                    net.post(now + cost + WIRE + ACROSS, (kind, k, 1 - c, d, 0))
            done = now + cost
            cost += 0.1 * (e["fini"] or e["finj"])
            if e["up"]:
                net.send(k, c, 1, done, ("U", k + 1, lanes[a, k + 1], a, 0))
            if e["dn"]:
                net.send(k, c, -1, done, ("V", k - 1, lanes[a, k - 1], a, 0))
            events[k, c].append(e)
            now += cost
            if kind == "D":
                for x in sorted(range(len(pairs)), key=lambda x: (x not in ride, x)):
                    if ends(x) == (i, j):
                        ready.add((x, k))
                        if k == 0 < j and x not in high:
                            now = handle(k, c, x, "up", now)
                        if k == n - 1 > i and x not in low:
                            now = handle(k, c, x, "down", now)
            busy[k, c] = now
            return now

        while net.queue:
            now, _, (kind, k, c, a, _) = heapq.heappop(net.queue)
            if kind == "wire":
                net.serve(k, c, now)
                continue
            if kind != "go":
                i, j = ends(a)
                last = k == (j if kind == "U" else i) and a not in ride
                waiting[k, c].append((now + PATIENCE * last, a, kind))
            if busy[k, c] > now + 1e-9:
                continue
            todo = order[k, c]
            more = made[k, c] < len(todo)
            hit = min((
                w for w in waiting[k, c]
                if (w[1], k) in ready and all((d, k) in ready or lanes[d, k] != c for d in ride.get(w[1], ()))
            ), default=None)
            if hit is not None and hit[0] + SLACK * more <= now + 1e-9:
                waiting[k, c].remove(hit)
                net.post(handle(k, c, hit[1], hit[2], now), ("go", k, c, -1, 0))
            elif more:
                made[k, c] += 1
                net.post(handle(k, c, todo[made[k, c] - 1], "D", now), ("go", k, c, -1, 0))
            elif hit is not None:
                net.post(hit[0], ("go", k, c, -1, 0))
        return events, max(busy.values())

    order = {}
    for k in range(n):
        for c in range(cores):
            def rank(a, k=k):
                i, j = ends(a)
                return min(n - 1 - j + k, i + n - 1 - k), any(ends(x) == (i, j) for x in ride), a
            first = [a for a in range(len(pairs)) if all(ends(x) != ends(a) for x in range(a))]
            order[k, c] = sorted((a for a in first if lanes[a, k] == c), key=rank)
    return run(order)


def plans(n, per, half, cores):
    pairs = tile_pairs(n * per, REACH)
    count = len(pairs)
    ride = riders(pairs, n, per, half, cores)
    lanes = lanes_of(pairs, n, per, half, cores, ride)
    own, gather, ends = gather_plan(pairs, n, per, half, cores, lanes, ride)
    scatter, _ = scatter_plan(pairs, n, per, half, cores, lanes, ride, [
        end + EXCHANGE + LAG * (k in (0, n - 1)) for k, end in enumerate(ends)
    ])

    def landings(plan, which):
        uses = {}
        for place, line in plan.items():
            for e in line:
                a = which(e)
                if a is not None:
                    uses.setdefault(a, set()).add(place)
        chosen = colours(uses)
        return chosen, max(chosen.values(), default=-1) + 1

    first_a, size_a = landings(
        gather, lambda e: e["other"] if e["lift"] else e["a"] if e["wait"] and not e["second"] else None
    )
    first_b, size_b = landings(gather, lambda e: e["a"] if e["wait"] and e["second"] and not e["lift"] else None)
    first_u, size_u = landings(scatter, lambda e: e["a"] if e["wait"] and e["u"] else None)
    first_v, size_v = landings(scatter, lambda e: e["a"] if e["wait"] and e["v"] else None)

    def word(a, k, flags):
        p, q = pairs[a]
        code = a | p << 8 | q << 13
        for bit, flag in enumerate(flags):
            code |= int(flag) << (18 + bit)
        if k < n - 1:
            code |= lanes[a, k + 1] << 28
        if k > 0:
            code |= lanes[a, k - 1] << 29
        return code

    def ag_sem(a, twin):
        return size_a + first_b.get(a, 0) if twin else first_a.get(a, 0)

    def rs_sem(a, turned):
        return size_u + first_v.get(a, 0) if turned else first_u.get(a, 0)

    def gather_sems(e):
        waits = ag_sem(e["other"], 0) if e["lift"] else ag_sem(e["a"], e["second"])
        sends = ag_sem(e["a"], 0 if e["cup"] or e["cdn"] or e["fup"] else e["second"])
        return waits | sends << 8 | e["other"] << 16 | e["lower"] << 24 | e["ride"] << 25 | e["lift"] << 26 | e["rest"] << 27

    def scatter_sems(e):
        turned = int(e["dn"] or not e["up"] and e["v"])
        sends = rs_sem(e["other"] if e["side"] else e["a"], turned)
        return rs_sem(e["a"], e["v"]) | sends << 8 | e["other"] << 16 | e["mean"] << 24 | e["second"] << 25

    def pad(lines):
        longest = max(len(line) for line in lines)
        return [line + [(0, 0)] * (longest - len(line)) for line in lines], [len(line) for line in lines]

    places, slots, sends, second, third, ag_sent, rs_sent = [(k, c) for k in range(n) for c in range(cores)], [], [], [], [], [], []
    for k, c in places:
        held = {(row, col): a + count * twin for a, twin, row, col, *_ in own[k, c]}
        slots.append([
            held.get((row, col), 3 * count + row * half + col) for row in range(per) for col in range(half)
        ])
        sends.append([
            (word(a, k, (twin, up, down, side)), ag_sem(a, twin)) for a, twin, _, _, up, down, side in own[k, c]
            if up or down or side
        ])
        second.append([
            (word(e["a"], k, [
                e[f] for f in ("wait", "second", "fup", "fdn", "merge", "cup", "cdn", "comp", "run", "blend")
            ]), gather_sems(e))
            for e in gather[k, c]
        ])
        third.append([
            (word(e["a"], k, [
                e[f] for f in ("comp", "first", "wait", "v", "up", "dn", "fini", "finj", "blend", "side")
            ]), scatter_sems(e))
            for e in scatter[k, c]
        ])
        ag_sent.append(sum(int(up) + int(down) + int(side) for *_, up, down, side in own[k, c])
                       + sum(e["fup"] + e["fdn"] + e["cup"] + e["cdn"] for e in gather[k, c]))
        rs_sent.append(sum(e["up"] + e["dn"] + e["side"] for e in scatter[k, c]))
    return dict(
        count=count, slots=slots, sends=pad(sends), gather=pad(second), scatter=pad(third),
        ag_sent=ag_sent, rs_sent=rs_sent, ag_sems=size_a + size_b, rs_sems=size_u + size_v,
    )


def make_tile_kernel(n, nf, ns, rows, cols, ne, vox_local, n_blocks, regions):
    per = rows // LANES
    half = cols // LANES
    peers = nf * ns
    plan = plans(n, per, half, ns)
    count = plan["count"]
    held = per * half

    def kernel(
        res, green, active_in, aperture, gain, region_in, strength_in, out,
        active, region, strength, sem_small,
        gv, act_col, buf, blocks, rests, img, ar_send, ar_land,
        wgt, dacc, total, stage, land,
        sem_g, sem_own, ag_s, ag_r, ar_s, ar_r, rs_s, rs_r,
    ):
        z = lax.axis_index("vox")
        f = lax.axis_index("freq")
        s = lax.axis_index("sub")
        has_up = z < n - 1
        has_down = z > 0
        z_up = jnp.minimum(z + 1, n - 1)
        z_down = jnp.maximum(z - 1, 0)

        def remote(src, dst, send, recv, target):
            return pltpu.make_async_remote_copy(
                src_ref=src, dst_ref=dst, send_sem=send, recv_sem=recv,
                device_id=target, device_id_type=MESH,
            )

        def above(code):
            return {"vox": z_up, "sub": (code >> 28) & 1}

        def below(code):
            return {"vox": z_down, "sub": (code >> 29) & 1}

        def peer(k):
            df, ds = k // ns, k % ns
            return {"freq": lax.rem(f + df, nf), "sub": lax.rem(s + ds, ns)}

        partner = {"sub": lax.rem(s + 1, ns)}

        def has(code, bit):
            return ((code >> (18 + bit)) & 1) == 1

        def lines(t):
            return pl.ds(pl.multiple_of(t * LANES, LANES), LANES)

        role = z * ns + s
        is_role = [role == r for r in range(n * ns)]

        def pick(values):
            usual = max(set(values), key=values.count)
            out_value = jnp.int32(usual)
            for r, value in enumerate(values):
                if value != usual:
                    out_value = jnp.where(is_role[r], jnp.int32(value), out_value)
            return out_value

        def table(lines):
            words, lengths = lines
            columns = [
                [pick([line[e][part] for line in words]) for e in range(len(words[0]))] for part in (0, 1)
            ]

            def at(e):
                found = []
                for level in columns:
                    bit = 0
                    while len(level) > 1:
                        odd = ((e >> bit) & 1) == 1
                        paired = [jnp.where(odd, b, a) for a, b in zip(level[::2], level[1::2])]
                        level, bit = paired + level[len(level) & ~1:], bit + 1
                    found.append(level[0])
                return found

            return at, pick(lengths)

        def drain(sem, sent):
            mine = pick(sent)
            for m in sorted(set(sent)):
                @pl.when(mine == m)
                def _(m=m):
                    block = buf.at[pl.ds(0, m)]
                    remote(block, block, sem, ag_r.at[0], {"vox": z_up}).wait_send()

        barrier = pltpu.get_barrier_semaphore()
        for k in range(1, peers):
            pl.semaphore_signal(barrier, inc=1, device_id=peer(k), device_id_type=MESH)
        for c in range(ns):
            @pl.when(has_up)
            def _():
                pl.semaphore_signal(barrier, inc=1, device_id={"vox": z_up, "sub": c}, device_id_type=MESH)

            @pl.when(has_down)
            def _():
                pl.semaphore_signal(barrier, inc=1, device_id={"vox": z_down, "sub": c}, device_id_type=MESH)

        green_copy = pltpu.make_async_copy(green, gv, sem_g)
        small = [
            pltpu.make_async_copy(a, b, sem_small.at[i])
            for i, (a, b) in enumerate((
                (active_in, active), (region_in, region), (strength_in, strength),
            ))
        ]
        for t in range(held):
            row, col = t // half * LANES, t % half * LANES
            pltpu.make_async_copy(
                res.at[row:row + LANES, col:col + LANES], buf.at[pick([line[t] for line in plan["slots"]])], sem_own
            ).start()
        for c in small:
            c.start()
        green_copy.start()
        own_at, n_own = table(plan["sends"])
        gather_at, n_gather = table(plan["gather"])
        scatter_at, n_scatter = table(plan["scatter"])
        out[...] = jnp.zeros_like(out)
        img[...] = jnp.zeros_like(img)
        blocks[...] = jnp.zeros_like(blocks)
        rests[...] = jnp.zeros_like(rests)
        pl.semaphore_wait(barrier, peers - 1 + ns * has_up.astype(jnp.int32) + ns * has_down.astype(jnp.int32))

        pltpu.make_async_copy(buf.at[pl.ds(0, held)], buf.at[pl.ds(held, held)], sem_own).wait()

        def ag_send(source, target, sem, side):
            remote(buf.at[source], buf.at[target], ag_s, ag_r.at[sem], side).start()

        @pl.loop(0, n_own)
        def _(e):
            code, sem = own_at(e)
            slot = (code & 255) + count * ((code >> 18) & 1)

            @pl.when(has(code, 1))
            def _():
                ag_send(slot, slot, sem, above(code))

            @pl.when(has(code, 2))
            def _():
                ag_send(slot, slot, sem, below(code))

            @pl.when(has(code, 3))
            def _():
                ag_send(slot, slot, sem, partner)

        for c in small:
            c.wait()
        for i in range(ne // LANES):
            line = active[0:1, i * LANES:(i + 1) * LANES].astype(jnp.float32)
            act_col[i * LANES:(i + 1) * LANES, :] = jnp.broadcast_to(line, (LANES, LANES)).T

        def pair_mask(row_tile, col_tile):
            rr = lax.broadcasted_iota(jnp.int32, (LANES, LANES), 0) + row_tile * LANES
            cc = lax.broadcasted_iota(jnp.int32, (LANES, LANES), 1) + col_tile * LANES
            in_band = jnp.abs(rr - cc) <= aperture[0]
            row_on = act_col[lines(row_tile), :] > 0.5
            col_on = active[0:1, lines(col_tile)] > 0
            return in_band & row_on & col_on

        def block_of(p, q):
            return lax.div(p, per) * n + lax.div(q, per)

        def inside(p, q):
            return lines(lax.rem(p, per)), lines(lax.rem(q, per))

        def block_rows(p):
            return pl.ds(pl.multiple_of(lax.div(p, per) * rows, rows), rows)

        def place(p, q):
            value = jnp.where(pair_mask(p, q), total[...], 0.0)
            high = value.astype(jnp.bfloat16)
            rr, cc = inside(p, q)
            blocks[block_of(p, q), rr, cc] = high
            rests[block_of(p, q), rr, cc] = (value - high.astype(jnp.float32)).astype(jnp.bfloat16)

        def image_part(p, q, rest):
            for v in range(vox_local // CHUNK):
                vs = pl.ds(v * CHUNK, CHUNK)
                g = gv[block_rows(q), vs]
                y = jnp.dot(blocks[block_of(p, q)], g, preferred_element_type=jnp.float32)
                if rest:
                    y = y + jnp.dot(rests[block_of(p, q)], g, preferred_element_type=jnp.float32)
                y = y * gv[block_rows(p), vs].astype(jnp.float32)
                img[:, vs] += jnp.sum(y.reshape(rows // 8, 8, CHUNK), axis=0)

        green_copy.wait()
        shape = (LANES, LANES)
        side_of = lax.broadcasted_iota(jnp.int32, shape, 0) - lax.broadcasted_iota(jnp.int32, shape, 1)

        @pl.loop(0, n_gather)
        def _(e):
            code, sems = gather_at(e)
            a, p, q = code & 255, (code >> 8) & 31, (code >> 13) & 31
            slot = a + count * ((code >> 19) & 1)
            merged = a + 2 * count
            other = (sems >> 16) & 255
            lower = (sems >> 24) & 1
            lift = (sems >> 26) & 1
            landed = jnp.where(lift == 1, other, slot)
            sem = (sems >> 8) & 255

            @pl.when(has(code, 0))
            def _():
                remote(buf.at[landed], buf.at[landed], ag_s, ag_r.at[sems & 255], above(code)).wait_recv()

            @pl.when(lift == 1)
            def _():
                both = buf[other].astype(jnp.float32)
                pairs = jnp.where(side_of == 0, both, both + both.T)
                away = side_of * (1 - 2 * lower) > 0
                buf[slot] = jnp.where(away, buf[slot].astype(jnp.float32), pairs).astype(jnp.bfloat16)

            @pl.when(((sems >> 25) & 1) == 1)
            def _():
                kept = side_of * (1 - 2 * lower) <= 0
                buf[a] = jnp.where(kept, buf[other + count * lower].astype(jnp.float32), 0.0).astype(jnp.bfloat16)

            @pl.when(has(code, 2))
            def _():
                ag_send(slot, slot, sem, above(code))

            @pl.when(has(code, 3))
            def _():
                ag_send(slot, slot, sem, below(code))

            @pl.when(has(code, 4))
            def _():
                one = buf[a].astype(jnp.float32)
                two = buf[a + count].astype(jnp.float32).T
                passing = (side_of <= 0) & has(code, 9)
                from_two = side_of * 0 + lower > 0
                both = jnp.where(passing, jnp.where(from_two, two, one), one + two)
                buf[merged] = both.astype(jnp.bfloat16)
                total[...] = both

                @pl.when(has(code, 5))
                def _():
                    ag_send(merged, a, sem, above(code))

                @pl.when(has(code, 6))
                def _():
                    ag_send(merged, a, sem, below(code))

            @pl.when(has(code, 7))
            def _():
                @pl.when(jnp.logical_not(has(code, 4)))
                def _():
                    total[...] = buf[a].astype(jnp.float32)
                place(p, q)

            exact = ((sems >> 27) & 1) == 1

            @pl.when(has(code, 8) & exact)
            def _():
                image_part(p, q, True)

            @pl.when(has(code, 8) & jnp.logical_not(exact))
            def _():
                image_part(p, q, False)

        for b in range(n_blocks):
            ar_send[b:b + 1, :] = jnp.sum(img[:, b * BLOCK:(b + 1) * BLOCK], axis=0, keepdims=True)
        exchanges = [
            remote(ar_send, ar_land.at[k], ar_s.at[k - 1], ar_r.at[k - 1], peer(k)) for k in range(1, peers)
        ]
        for e in exchanges:
            e.start()
        strength_map = jnp.concatenate(
            [jnp.full((1, BLOCK), strength[region[b]], jnp.float32) for b in range(n_blocks)], axis=0
        )

        drain(ag_s, plan["ag_sent"])
        for e in exchanges:
            e.wait_recv()
        image = ar_send[...]
        for k in range(1, peers):
            image = image + ar_land[k]
        scaled = penalize(image, strength_map)
        for b in range(n_blocks):
            img[0:1, b * BLOCK:(b + 1) * BLOCK] = scaled[b:b + 1, :]

        lane_of = lax.broadcasted_iota(jnp.int32, (8, LANES), 1)
        in_head = (lax.broadcasted_iota(jnp.int32, (8, LANES), 0) == 0) & (lane_of < 8)
        head_lane = lax.broadcasted_iota(jnp.int32, (1, LANES), 1)

        def encode(value, power=None):
            if power is None:
                largest = jnp.max(jnp.max(jnp.abs(value), axis=0, keepdims=True), axis=1, keepdims=True)
                power = jnp.floor(jnp.log(jnp.maximum(largest, 1e-36)) * (1 / LN2)) + 1.0
            scaled = value * (STEPS * jnp.exp(power * -LN2))
            code = (scaled + jnp.where(scaled >= 0, 0.5, -0.5)).astype(jnp.int32)
            bits = jnp.broadcast_to((power + 128.0).astype(jnp.int32), (8, LANES))
            head = (code[0:8, :] & -2) | ((bits >> jnp.minimum(lane_of, 8)) & 1)
            head = jnp.where(in_head, head, code[0:8, :])
            return jnp.concatenate([head, code[8:, :]], axis=0).astype(jnp.int16)

        def decode(slot):
            code = land[slot].astype(jnp.int32)
            bits = jnp.where(head_lane < 8, (code[0:1, :] & 1) << jnp.minimum(head_lane, 8), 0)
            power = jnp.sum(bits.astype(jnp.float32), axis=1, keepdims=True) - 128.0
            return code.astype(jnp.float32) * (jnp.exp(power * LN2) * (1 / STEPS)), power

        def scatter(slot, sem, target):
            return remote(stage.at[slot], land.at[slot], rs_s, rs_r.at[sem], target)

        @pl.loop(0, n_scatter)
        def _(e):
            code, sems = scatter_at(e)
            a, p, q = code & 255, (code >> 8) & 31, (code >> 13) & 31
            turned = (code >> 21) & 1
            slot = a + count * turned
            other = (sems >> 16) & 255
            wait_sem = sems & 255
            sem = (sems >> 8) & 255

            block = block_of(p, q)
            rr, cc = inside(p, q)

            def weigh(part):
                wgt[part, :] = (gv[part, :].astype(jnp.float32) * img[0:1, :]).astype(jnp.bfloat16)

            @pl.when(has(code, 1))
            def _():
                weigh(block_rows(q))

            @pl.when(((sems >> 25) & 1) == 1)
            def _():
                weigh(block_rows(p))

            def product(left, right):
                return lax.dot_general(left, right, (((1,), (1,)), ((), ())), preferred_element_type=jnp.float32)

            @pl.when(has(code, 0))
            def _():
                dacc[block] = product(gv[block_rows(p), :], wgt[block_rows(q), :])

            @pl.when(((sems >> 24) & 1) == 1)
            def _():
                dacc[block] = 0.5 * (dacc[block] + product(wgt[block_rows(p), :], gv[block_rows(q), :]))

            @pl.when(has(code, 2))
            def _():
                scatter(slot, wait_sem, above(code)).wait_recv()

            @pl.when(has(code, 4) | has(code, 5))
            def _():
                total[...] = dacc[block, rr, cc]

                @pl.when(has(code, 8))
                def _():
                    d = jnp.where(has(code, 4), q, p)
                    dr, dc = inside(d, d)
                    total[...] = jnp.where(side_of > 0, total[...], dacc[block_of(d, d), dr, dc])

                @pl.when(has(code, 2))
                def _():
                    total[...] += decode(slot)[0]

                stage[slot] = encode(total[...])

            @pl.when(has(code, 4))
            def _():
                scatter(slot, sem, above(code)).start()

            @pl.when(has(code, 5))
            def _():
                scatter(slot, sem, below(code)).start()

            @pl.when(has(code, 9))
            def _():
                both, power = decode(slot)
                mirrored = jnp.where(side_of <= 0, both, both.T)
                aside = other + count * turned
                stage[aside] = encode(mirrored, power)
                scatter(aside, sem, partner).start()

            @pl.when(has(code, 6) | has(code, 7))
            def _():
                total[...] = dacc[block, rr, cc]

                @pl.when(has_down)
                def _():
                    total[...] += decode(a)[0]

                @pl.when(has_up)
                def _():
                    total[...] += decode(a + count)[0]

            @pl.when(has(code, 6))
            def _():
                new = buf[a].astype(jnp.float32) - gain[0] * total[...]
                out[lines(lax.rem(p, per)), lines(lax.rem(q, half))] = jnp.where(pair_mask(p, q), new, 0.0)

            @pl.when(has(code, 7))
            def _():
                new = buf[a + count].astype(jnp.float32) - gain[0] * total[...].T
                out[lines(lax.rem(q, per)), lines(lax.rem(p, half))] = jnp.where(pair_mask(q, p), new, 0.0)

        for e in exchanges:
            e.wait_send()

        drain(rs_s, plan["rs_sent"])

    dma = pltpu.SemaphoreType.DMA
    tile16 = lambda m: pltpu.VMEM((m, LANES, LANES), jnp.bfloat16)
    scratch = [
        pltpu.VMEM((1, ne), jnp.int32),
        pltpu.SMEM((n_blocks,), jnp.int32),
        pltpu.SMEM((regions,), jnp.float32),
        dma((3,)),
        pltpu.VMEM((ne, vox_local), jnp.bfloat16),
        pltpu.VMEM((ne, LANES), jnp.float32),
        tile16(3 * count + held),
        pltpu.VMEM((n * n, rows, rows), jnp.bfloat16),
        pltpu.VMEM((n * n, rows, rows), jnp.bfloat16),
        pltpu.VMEM((8, vox_local), jnp.float32),
        pltpu.VMEM((n_blocks, BLOCK), jnp.float32),
        pltpu.VMEM((peers, n_blocks, BLOCK), jnp.float32),
        pltpu.VMEM((ne, vox_local), jnp.bfloat16),
        pltpu.VMEM((n * n, rows, rows), jnp.float32),
        pltpu.VMEM((LANES, LANES), jnp.float32),
        pltpu.VMEM((2 * count, LANES, LANES), jnp.int16),
        pltpu.VMEM((2 * count, LANES, LANES), jnp.int16),
        dma, dma, dma, dma((plan["ag_sems"],)),
        dma((peers - 1,)), dma((peers - 1,)),
        dma, dma((plan["rs_sems"],)),
    ]
    return kernel, scratch


def make_kernel(n, nf, ns, rows, cols, ne, vox_local, n_blocks, regions):
    tile = min(rows, LANES)
    per = rows // tile
    col_tiles = cols // LANES
    vchunk = min(512, vox_local)
    peers = nf * ns

    def kernel(
        res, green, active_in, aperture_in, gain_in, region_in, strength_in, out,
        active, aperture, gain, region, strength, sem_small,
        allm, gv, act_col, mm, img, ar_send, ar_land, wgt, gacc, flipped, send_buf, land_r, land_l,
        sem_g, sem_own, agr_s, agr_r, agl_s, agl_r, ar_s, ar_r, rsr_s, rsr_r, rsl_s, rsl_r,
    ):
        z = lax.axis_index("vox")
        f = lax.axis_index("freq")
        s = lax.axis_index("sub")
        has_up = z < n - 1
        has_down = z > 0
        up = {"vox": jnp.minimum(z + 1, n - 1)}
        down = {"vox": jnp.maximum(z - 1, 0)}

        def row_of(block):
            return pl.multiple_of(block * rows, rows)

        small = [
            pltpu.make_async_copy(a, b, sem_small.at[i])
            for i, (a, b) in enumerate((
                (active_in, active), (aperture_in, aperture), (gain_in, gain),
                (region_in, region), (strength_in, strength),
            ))
        ]
        for c in small:
            c.start()
        own_copy = pltpu.make_async_copy(res, allm.at[pl.ds(row_of(z), rows), :], sem_own)
        own_copy.start()
        green_copy = pltpu.make_async_copy(green, gv, sem_g)
        green_copy.start()

        def peer(k):
            df, ds = k // ns, k % ns
            return {"freq": lax.rem(f + df, nf), "sub": lax.rem(s + ds, ns)}

        barrier = pltpu.get_barrier_semaphore()
        for k in range(1, peers):
            pl.semaphore_signal(barrier, inc=1, device_id=peer(k), device_id_type=MESH)

        @pl.when(has_up)
        def _():
            pl.semaphore_signal(barrier, inc=1, device_id=up, device_id_type=MESH)

        @pl.when(has_down)
        def _():
            pl.semaphore_signal(barrier, inc=1, device_id=down, device_id_type=MESH)

        pl.semaphore_wait(barrier, peers - 1 + has_up.astype(jnp.int32) + has_down.astype(jnp.int32))

        def square(q):
            local = q * tile - s * cols
            inside = (local >= 0) & (local < cols)
            return inside, lax.div(jnp.clip(local, 0, cols - 1), LANES)

        def band(q, kind):
            reach = q * tile - s * cols + ne
            shift = ne // LANES + APERTURE_MAX // LANES + 1
            lift = LANES * (shift - ne // LANES)
            first = lax.div(reach + lift - APERTURE_MAX, LANES) - shift
            last = lax.div(reach + lift + tile - 1 + APERTURE_MAX, LANES) - shift + 1
            first = jnp.clip(first, 0, col_tiles)
            last = jnp.clip(last, 0, col_tiles)
            if kind != FULL:
                inside, diag = square(q)
            if kind == UP:
                last = jnp.where(inside, jnp.minimum(last, diag + 1), last)
            if kind == DOWN:
                first = jnp.where(inside, jnp.maximum(first, diag), first)
            return first, last - first

        def per_width(q, fn, kind=FULL):
            first, count = band(q, kind)
            for w in range(1, col_tiles + 1):
                @pl.when(count == w)
                def _(w=w):
                    fn(pl.ds(pl.multiple_of(first * LANES, LANES), w * LANES))

        def tile_rows(q):
            return pl.ds(pl.multiple_of(q * tile, tile), tile)

        def remote(src, dst, send, recv, target):
            return pltpu.make_async_remote_copy(
                src_ref=src, dst_ref=dst, send_sem=send, recv_sem=recv,
                device_id=target, device_id_type=MESH,
            )

        def each_tile(block, make, act, kind=FULL):
            for t in range(per):
                q = block * per + t
                per_width(q, lambda c, q=q: act(make(q, c)), kind)

        def gather_up(q, c):
            a = allm.at[tile_rows(q), c]
            return remote(a, a, agr_s.at[q], agr_r.at[q], up)

        def gather_down(q, c):
            a = allm.at[tile_rows(q), c]
            return remote(a, a, agl_s.at[q], agl_r.at[q], down)

        for t in range(per):
            q = z * per + t

            def first_up(c, q=q, t=t):
                remote(res.at[pl.ds(t * tile, tile), c], allm.at[tile_rows(q), c],
                       agr_s.at[q], agr_r.at[q], up).start()

            def first_down(c, q=q, t=t):
                remote(res.at[pl.ds(t * tile, tile), c], allm.at[tile_rows(q), c],
                       agl_s.at[q], agl_r.at[q], down).start()

            @pl.when(has_up)
            def _():
                per_width(q, first_up)

            @pl.when(has_down)
            def _():
                per_width(q, first_down)

        for c in small:
            c.wait()
        for i in range(ne // LANES):
            line = active[0:1, i * LANES:(i + 1) * LANES].astype(jnp.float32)
            act_col[i * LANES:(i + 1) * LANES, :] = jnp.broadcast_to(line, (LANES, LANES)).T
        img[...] = jnp.zeros_like(img)
        col0 = pl.multiple_of(s * cols, cols)

        def pair_mask(block):
            r0 = row_of(block)
            rr = lax.broadcasted_iota(jnp.int32, (rows, cols), 0) + r0
            cc = lax.broadcasted_iota(jnp.int32, (rows, cols), 1) + col0
            in_band = jnp.abs(rr - cc) <= aperture[0]
            row_on = act_col[pl.ds(r0, rows), 0:1] > 0.5
            col_on = active[0:1, pl.ds(col0, cols)] > 0
            return in_band & row_on & col_on

        def image_part(block):
            r0 = row_of(block)
            value = allm[pl.ds(r0, rows), :].astype(jnp.float32)
            mm[...] = jnp.where(pair_mask(block), value, 0.0).astype(jnp.bfloat16)

            @pl.loop(0, vox_local // vchunk)
            def _(v):
                vs = pl.ds(pl.multiple_of(v * vchunk, vchunk), vchunk)
                y = jnp.dot(mm[...], gv[pl.ds(col0, cols), vs], preferred_element_type=jnp.float32)
                y = y * gv[pl.ds(r0, rows), vs].astype(jnp.float32)
                img[:, vs] += jnp.sum(y.reshape(rows // 8, 8, vchunk), axis=0)

        own_copy.wait()
        green_copy.wait()
        image_part(z)

        @pl.loop(0, n - 1)
        def _(step):
            from_below = z - 1 - step
            from_above = z + 1 + step
            for t in range(per):
                @pl.when(from_below >= 0)
                def _():
                    q = from_below * per + t

                    def land(c):
                        gather_up(q, c).wait_recv()

                        @pl.when(has_up)
                        def _():
                            gather_up(q, c).start()
                    per_width(q, land)

                @pl.when(from_above < n)
                def _():
                    q = from_above * per + t

                    def land(c):
                        gather_down(q, c).wait_recv()

                        @pl.when(has_down)
                        def _():
                            gather_down(q, c).start()
                    per_width(q, land)

            @pl.when(from_below >= 0)
            def _():
                image_part(from_below)

            @pl.when(from_above < n)
            def _():
                image_part(from_above)

        ar_send[...] = jnp.sum(img[...], axis=0, keepdims=True)
        exchanges = [
            remote(ar_send, ar_land.at[k], ar_s.at[k], ar_r.at[k], peer(k)) for k in range(1, peers)
        ]
        for e in exchanges:
            e.start()
        strength_map = jnp.concatenate(
            [jnp.full((1, BLOCK), strength[region[b]], jnp.float32) for b in range(n_blocks)], axis=1
        )

        @pl.loop(0, n)
        def _(b):
            @pl.when(has_up & (b <= z))
            def _():
                each_tile(b, gather_up, lambda c: c.wait_send())

            @pl.when(has_down & (b >= z))
            def _():
                each_tile(b, gather_down, lambda c: c.wait_send())

        for e in exchanges:
            e.wait_recv()
        total = ar_send[...]
        for k in range(1, peers):
            total = total + ar_land[k]
        img[0:1, :] = penalize(total, strength_map)

        wrows = 32

        @pl.loop(0, cols // wrows)
        def _(i):
            src = pl.ds(pl.multiple_of(col0 + i * wrows, wrows), wrows)
            dst = pl.ds(pl.multiple_of(i * wrows, wrows), wrows)
            wgt[dst, :] = (gv[src, :].astype(jnp.float32) * img[0:1, :]).astype(jnp.bfloat16)

        def scatter_up(q, c):
            return remote(send_buf.at[tile_rows(q), c], land_r.at[tile_rows(q), c],
                          rsr_s.at[q], rsr_r.at[q], up)

        def scatter_down(q, c):
            return remote(send_buf.at[tile_rows(q), c], land_l.at[tile_rows(q), c],
                          rsl_s.at[q], rsl_r.at[q], down)

        def partial_step(k, ends):
            lo, hi = ends
            use_hi = (hi > z) & ((lo >= z) | (z + (n - 1 - hi) <= (n - 1 - z) + lo))
            d = jnp.where(use_hi, hi, lo)
            rs = pl.ds(row_of(d), rows)
            part = lax.dot_general(
                gv[rs, :], wgt[...], (((1,), (1,)), ((), ())), preferred_element_type=jnp.float32
            )
            gacc[rs, :] = part
            sends_up = (d > z) & jnp.logical_not(has_down)
            sends_down = (d < z) & jnp.logical_not(has_up)

            @pl.when(sends_up | sends_down)
            def _():
                send_buf[rs, :] = part.astype(jnp.bfloat16)

            @pl.when(sends_up)
            def _():
                each_tile(d, scatter_up, lambda c: c.start(), UP)

            @pl.when(sends_down)
            def _():
                each_tile(d, scatter_down, lambda c: c.start(), DOWN)

            step_hi = use_hi.astype(jnp.int32)
            return lo + 1 - step_hi, hi - step_hi

        lax.fori_loop(0, n, partial_step, (jnp.int32(0), jnp.int32(n - 1)))

        @pl.loop(0, n - 1)
        def _(slot):
            @pl.when(has_down & (slot >= z))
            def _():
                d = z + n - 1 - slot
                for t in range(per):
                    q = d * per + t

                    def add(c):
                        scatter_up(q, c).wait_recv()
                        send_buf[tile_rows(q), c] = (
                            gacc[tile_rows(q), c] + land_r[tile_rows(q), c].astype(jnp.float32)
                        ).astype(jnp.bfloat16)
                        scatter_up(q, c).start()
                    per_width(q, add, UP)

            @pl.when(has_up & (slot >= n - 1 - z))
            def _():
                d = slot - (n - 1 - z)
                for t in range(per):
                    q = d * per + t

                    def add(c):
                        scatter_down(q, c).wait_recv()
                        send_buf[tile_rows(q), c] = (
                            gacc[tile_rows(q), c] + land_l[tile_rows(q), c].astype(jnp.float32)
                        ).astype(jnp.bfloat16)
                        scatter_down(q, c).start()
                    per_width(q, add, DOWN)

        @pl.when(has_down)
        def _():
            each_tile(z, scatter_up, lambda c: c.wait_recv(), UP)

        @pl.when(has_up)
        def _():
            each_tile(z, scatter_down, lambda c: c.wait_recv(), DOWN)

        mine = pl.ds(row_of(z), rows)
        def add_landed(land, there, q, mirrored):
            inside, diag = square(q)
            offset = lax.rem(q * tile, LANES)
            for j in range(col_tiles):
                c = slice(j * LANES, (j + 1) * LANES)
                flip = inside & mirrored(j, diag)

                @pl.when(there & jnp.logical_not(flip))
                def _():
                    gacc[tile_rows(q), c] += land[tile_rows(q), c].astype(jnp.float32)

                @pl.when(there & flip)
                def _():
                    twin = pl.ds(pl.multiple_of(col0 + j * LANES, LANES), LANES)
                    own = pl.ds(pl.multiple_of(diag * LANES, LANES), LANES)
                    flipped[...] = land[twin, own].astype(jnp.float32).T
                    gacc[tile_rows(q), c] += flipped[pl.ds(pl.multiple_of(offset, tile), tile), :]

        for t in range(per):
            add_landed(land_r, has_down, z * per + t, lambda j, diag: j > diag)
            add_landed(land_l, has_up, z * per + t, lambda j, diag: j < diag)
        gradient = gacc[mine, :]
        data = allm[mine, :].astype(jnp.float32)
        out[...] = jnp.where(pair_mask(z), data - gain[0] * gradient, 0.0)

        for e in exchanges:
            e.wait_send()

        @pl.loop(0, n)
        def _(b):
            @pl.when(has_up & (b > z))
            def _():
                each_tile(b, scatter_up, lambda c: c.wait_send(), UP)

            @pl.when(has_down & (b < z))
            def _():
                each_tile(b, scatter_down, lambda c: c.wait_send(), DOWN)

    tiles = n * per
    dma = pltpu.SemaphoreType.DMA
    scratch = [
        pltpu.VMEM((1, ne), jnp.int32),
        pltpu.SMEM((1,), jnp.int32),
        pltpu.SMEM((1,), jnp.float32),
        pltpu.SMEM((n_blocks,), jnp.int32),
        pltpu.SMEM((regions,), jnp.float32),
        dma((5,)),
        pltpu.VMEM((ne, cols), jnp.bfloat16),
        pltpu.VMEM((ne, vox_local), jnp.bfloat16),
        pltpu.VMEM((ne, LANES), jnp.float32),
        pltpu.VMEM((rows, cols), jnp.bfloat16),
        pltpu.VMEM((8, vox_local), jnp.float32),
        pltpu.VMEM((1, vox_local), jnp.float32),
        pltpu.VMEM((peers, 1, vox_local), jnp.float32),
        pltpu.VMEM((cols, vox_local), jnp.bfloat16),
        pltpu.VMEM((ne, cols), jnp.float32),
        pltpu.VMEM((LANES, LANES), jnp.float32),
        pltpu.VMEM((ne, cols), jnp.bfloat16),
        pltpu.VMEM((ne, cols), jnp.bfloat16),
        pltpu.VMEM((ne, cols), jnp.bfloat16),
        dma, dma,
        dma((tiles,)), dma((tiles,)), dma((tiles,)), dma((tiles,)),
        dma((peers,)), dma((peers,)),
        dma((tiles,)), dma((tiles,)), dma((tiles,)), dma((tiles,)),
    ]
    return kernel, scratch


def tiled(sizes, rows, cols, ne, vox_local):
    n, ns = sizes["vox"], sizes["sub"]
    return (
        rows % LANES == 0 and vox_local % CHUNK == 0 and rows * n == ne and cols * ns == ne
        and n > 1 and ns > 1 and cols % rows == 0 and ne // LANES <= 32
        and len(tile_pairs(ne // LANES, REACH)) <= 256
    )


def solution(mesh):
    sizes = dict(mesh.shape)

    def body(residual, green, active, aperture, step_gain, block_region, strength):
        _, rows, cols = residual.shape
        _, ne, vox_local = green.shape
        tiles = tiled(sizes, rows, cols, ne, vox_local)
        make = make_tile_kernel if tiles else make_kernel
        kernel, scratch = make(
            sizes["vox"], sizes["freq"], sizes["sub"], rows, cols, ne, vox_local,
            block_region.shape[0], strength.shape[0],
        )
        vmem = pl.BlockSpec(memory_space=pltpu.VMEM)
        hbm = pl.BlockSpec(memory_space=pltpu.HBM)
        updated = pl.pallas_call(
            kernel,
            out_shape=jax.ShapeDtypeStruct((rows, cols), jnp.float32),
            in_specs=[hbm] * 3 + [pl.BlockSpec(memory_space=pltpu.SMEM) if tiles else hbm] * 2 + [hbm] * 2,
            out_specs=vmem,
            scratch_shapes=scratch,
            compiler_params=pltpu.CompilerParams(
                collective_id=0, has_side_effects=True, vmem_limit_bytes=32 * 1024 * 1024
            ),
            name="imaging_step",
        )(*[
            pltpu.with_memory_space_constraint(a, pltpu.HBM) if a.size > 1 else a
            for a in (residual[0], green[0], active, aperture, step_gain, block_region, strength)
        ])
        return updated[None]

    in_specs = (
        P(("groups", "freq"), "vox", "sub"),
        P(("groups", "freq"), None, "vox"),
        P(("groups", "freq"), None),
        P(("groups", "freq")),
        P(("groups", "freq")),
        P(("groups", "vox")),
        P(),
    )
    out_specs = P(("groups", "freq"), "vox", "sub")
    return jax.shard_map(body, mesh=mesh, in_specs=in_specs, out_specs=out_specs, check_vma=False)
```

```python
import heapq
import itertools

import jax
import jax.numpy as jnp
from jax import lax
from jax.experimental import pallas as pl
from jax.experimental.pallas import tpu as pltpu
from jax.sharding import PartitionSpec as P

BLOCK = 128
LANES = 128
APERTURE_MAX = 511
smooth_sq = 0.0625
FULL, UP, DOWN = range(3)
MESH = pl.DeviceIdType.MESH
REACH = (APERTURE_MAX + LANES - 1) // LANES
CHUNK = 512
LN2 = 0.6931471805599453
STEPS = 32600.0


def penalize(image_sum, strength_map):
    return image_sum - strength_map * image_sum / jnp.sqrt(image_sum * image_sum + smooth_sq)


WIRE, HOP_FIRST, HOP = 0.354, 2.3, 2.0
IMAGE, PLACE, MERGE, PARTIAL, WEIGHT, ADD = 0.47, 0.04, 0.1, 0.47, 0.2, 0.12
EXCHANGE, LAG, PATIENCE, SLACK, ACROSS = 2.8, 0.0, 1.0, 0.8, 1.0


def tile_pairs(tiles, reach):
    return [(p, q) for p in range(tiles) for q in range(p, min(tiles, p + reach + 1))]


def riders(pairs, n, per, half, cores):
    if cores != 2 or half != REACH or REACH % per or REACH * LANES <= APERTURE_MAX:
        return {}
    index = {pair: a for a, pair in enumerate(pairs)}
    return {a: (index[p, p], index[q, q]) for a, (p, q) in enumerate(pairs) if q - p == REACH}


def lanes_of(pairs, n, per, half, cores, ride):
    sizes = {}
    for p, q in pairs:
        sizes[p // per, q // per] = sizes.get((p // per, q // per), 0) + 1
    lanes = {}
    for k in range(n):
        load, follows, light = [0] * cores, {}, {}
        for a in ride:
            i, j = pairs[a][0] // per, pairs[a][1] // per
            for own, there in ((i, k > i), (j, k < j)):
                if there:
                    follows[own, own] = i, j
                    light[own, own] = light.get((own, own), 0) + 1

        def rank(block, k=k):
            i, j = block
            far = n - 1 - j if k == 0 else i if k == n - 1 else k not in block
            return far, k not in block, -sizes[block], block

        def weight(block, k=k, light=light):
            return (sizes[block] - light.get(block, 0)) * (block != (k, k) or 0 < k < n - 1)

        order = sorted(sizes, key=rank)
        forced = {(i, j): (j if k == i else i) * per // half for i, j in order if k in (i, j)}
        free = [block for block in order if block not in forced and block not in follows]

        def filled(where, follows=follows, forced=forced):
            return {**{block: where[to] for block, to in follows.items() if block not in forced}, **where}

        def unevenness(picks):
            where = filled({**forced, **dict(zip(free, picks))})
            total, worst = [0] * cores, []
            for at, block in enumerate(order):
                total[where[block]] += weight(block)
                if at + 1 == len(order) or rank(order[at + 1])[0] != rank(block)[0]:
                    worst.append(max(total) - min(total))
            return sum(worst), picks

        if cores ** len(free) <= 4096:
            chosen = dict(zip(free, min(map(unevenness, itertools.product(range(cores), repeat=len(free))))[1]))
        else:
            chosen = {}
            for block in free:
                chosen[block] = load.index(min(load))
                load[chosen[block]] += weight(block)
        chosen = filled({**forced, **chosen})
        for a, (p, q) in enumerate(pairs):
            lanes[a, k] = chosen[p // per, q // per]
    return lanes


def colours(uses):
    taken, chosen = {}, {}
    for a in sorted(uses, key=lambda a: (-len(uses[a]), a)):
        colour = 0
        while any(colour in taken.setdefault(place, set()) for place in uses[a]):
            colour += 1
        for place in uses[a]:
            taken[place].add(colour)
        chosen[a] = colour
    return chosen


class Network:
    def __init__(self, cores, hop):
        self.cores, self.hop, self.queue, self.count = cores, hop, [], 0
        self.wires = {}

    def post(self, time, what):
        self.count += 1
        heapq.heappush(self.queue, (time, self.count, what))

    def send(self, k, c, step, time, what):
        lines, turn, free = self.wires.setdefault((k, step), ([[] for _ in range(self.cores)], 0, 0.0))
        lines[c].append(what)
        self.post(max(time, free), ("wire", k, step, 0, 0))

    def serve(self, k, step, now):
        lines, turn, free = self.wires[k, step]
        if free > now + 1e-9:
            return
        for c in range(self.cores):
            line = lines[(turn + c) % self.cores]
            if line:
                self.post(now + WIRE + self.hop, line.pop(0))
                self.wires[k, step] = lines, (turn + c + 1) % self.cores, now + WIRE
                self.post(now + WIRE, ("wire", k, step, 0, 0))
                return


def gather_plan(pairs, n, per, half, cores, lanes, ride):
    net = Network(cores, HOP_FIRST)
    own, events = {}, {}
    seen, busy, missing = set(), {}, {}
    low = {pair[0]: a for a, pair in ride.items()}
    high = {pair[1]: a for a, pair in ride.items()}
    for p, q in pairs:
        for k in range(n):
            missing[p // per, q // per, k] = missing.get((p // per, q // per, k), 0) + 1

    def send(k, c, a, step, kind, now):
        net.send(k, c, step, now, (kind, k + step, lanes[a, k + step], a, 0))

    for k in range(n):
        for c in range(cores):
            own[k, c], events[k, c] = [], []
        mine = []
        for a, (p, q) in enumerate(pairs):
            i, j = p // per, q // per
            c = lanes[a, k]
            if i == k < j:
                mine.append((j - i, c, a, 0, q, 1, 0))
            elif i < k == j:
                mine.append((j - i, c, a, 1, p, 0, 1))
            elif i == j == k:
                mine.append((n, c, a, 0, q, int(p == q and a not in low), int(p == q and a not in high)))
                if p < q:
                    mine.append((n, c, a, 1, p, 0, 0))
        for _, c, a, second, other, up, down in sorted(mine):
            p, q = pairs[a]
            up, down = up and k < n - 1 and a not in ride, down and k > 0 and a not in ride
            side = a in low and k < n - 1 or a in high and k > 0
            own[k, c].append((a, second, (q if second else p) % per, other % half, up, down, side))
            if side:
                net.post(0.1 + WIRE + ACROSS, ("lift", k, 1 - c, a, 0))
            if up:
                send(k, c, a, 1, "A", 0.1)
            if down:
                send(k, c, a, -1, "B" if second else "A", 0.1)
        for c in range(cores):
            here = [a for a, (p, q) in enumerate(pairs) if p // per == q // per == k and lanes[a, k] == c]
            for a in sorted(here, key=lambda a: pairs[a][0] == pairs[a][1]):
                net.post(0.5, ("own", k, c, a, 0))
    while net.queue:
        now, _, (kind, k, c, a, _) = heapq.heappop(net.queue)
        if kind == "wire":
            net.serve(k, c, now)
            continue
        at = busy.get((k, c), 0.0)
        if at > now + 1e-9:
            net.post(at, (kind, k, c, a, 0))
            continue
        p, q = pairs[a]
        i, j = p // per, q // per
        e = dict(a=a, wait=int(kind != "own"), second=int(kind == "B"), fup=0, fdn=0, merge=0, cup=0, cdn=0, comp=0, run=0)
        e.update(blend=0, ride=0, lift=0, other=0, lower=0, rest=0)
        if kind == "lift":
            up = a in low
            e.update(a=low[a] if up else high[a], second=int(not up), fup=int(up), fdn=int(not up))
            e.update(lift=1, blend=1, other=a, lower=int(not up))
            a = e["a"]
        elif kind in ("rideA", "rideB"):
            e.update(wait=0, ride=1, comp=1, lower=int(kind == "rideB"), other=low[a] if k > i else high[a])
        elif kind == "own":
            e["comp"] = 1
            if p < q:
                e.update(merge=1, cup=int(k < n - 1), cdn=int(k > 0))
        elif j < k:
            e.update(fup=int(k < n - 1), comp=1)
        elif i > k:
            e.update(fdn=int(k > 0), comp=1)
        else:
            if kind == "A":
                e["fup"] = int(k < j)
            else:
                e["fdn"] = int(k > i)
            whole = k in (i, j) or (a, k) in seen
            seen.add((a, k))
            if whole:
                e.update(merge=1, comp=1, cup=int(k == j and k < n - 1), cdn=int(k == i and k > 0))
                e.update(blend=int(a in ride and k in (i, j)), lower=int(k == i))
        if a in ride and kind in ("A", "B"):
            if kind == "A" and k > i:
                net.post(now, ("rideA", k, c, ride[a][0], 0))
            if k < j and (kind == "B" or k < i):
                net.post(now, ("rideB" if kind == "B" else "rideA", k, c, ride[a][1], 0))
        for flag, step, sent in (("fup", 1, "A"), ("fdn", -1, "B" if e["second"] else "A"), ("cup", 1, "A"), ("cdn", -1, "A")):
            if e[flag]:
                send(k, c, a, step, sent, now + 0.05 + MERGE * e["merge"])
        if e["comp"]:
            block = pairs[a][0] // per, pairs[a][1] // per, k
            missing[block] -= 1
            e["run"] = int(missing[block] == 0)
            e["rest"] = int(e["run"] and block[0] <= k <= block[1])
        busy[k, c] = now + 0.06 + MERGE * (e["merge"] + e["ride"] + e["blend"] * (1 - e["merge"])) + PLACE * e["comp"] + IMAGE * e["run"]
        events[k, c].append(e)
    return own, events, [max(busy[k, c] for c in range(cores)) for k in range(n)]


def scatter_plan(pairs, n, per, half, cores, lanes, ride, starts):
    low = {pair[0]: a for a, pair in ride.items()}
    high = {pair[1]: a for a, pair in ride.items()}

    def ends(a):
        return pairs[a][0] // per, pairs[a][1] // per

    def run(order):
        net = Network(cores, HOP)
        events = {key: [] for key in order}
        busy, got, weighted, ready = {}, {}, set(), set()
        made = {key: 0 for key in order}
        waiting = {key: [] for key in order}
        for k, c in order:
            busy[k, c] = starts[k]
            net.post(starts[k], ("go", k, c, -1, 0))

        def handle(k, c, a, kind, now):
            i, j = ends(a)
            e = dict(a=a, comp=int(kind == "D"), first=0, wait=int(kind in ("U", "V")), v=int(kind in ("V", "down")))
            e.update(u=int(kind == "U"), up=0, dn=0, fini=0, finj=0, blend=0, side=0, other=0, mean=0, second=0)
            cost = ADD
            if kind == "D":
                e["first"] = int((j, k, c) not in weighted)
                weighted.add((j, k, c))
                e["mean"] = int(made[k, c] > 1 or 0 < k < n - 1)
                if e["mean"]:
                    e["second"] = int((i, k, c) not in weighted)
                    weighted.add((i, k, c))
                cost = PARTIAL * (1 + e["mean"]) + WEIGHT * (e["first"] + e["second"]) + 0.06
            elif not e["wait"]:
                e["up"], e["dn"] = int(kind == "up"), int(kind == "down")
            else:
                got.setdefault((a, k), set()).add(kind)
                e["up"], e["dn"] = int(kind == "U" and k < j), int(kind == "V" and k > i)
                need = int(0 < k <= j) + int(i <= k < n - 1)
                if k in (i, j) and len(got[a, k]) == need:
                    e.update(fini=int(k == i), finj=int(k == j and pairs[a][0] < pairs[a][1]))
            if a in ride:
                e["blend"] = int(e["up"] or e["dn"])
                if e["wait"] and k == (j if kind == "U" else i):
                    d = ride[a][kind == "U"]
                    e.update(side=1, other=d)
                    cost += 0.1
                    net.post(now + cost + WIRE + ACROSS, (kind, k, 1 - c, d, 0))
            done = now + cost
            cost += 0.1 * (e["fini"] or e["finj"])
            if e["up"]:
                net.send(k, c, 1, done, ("U", k + 1, lanes[a, k + 1], a, 0))
            if e["dn"]:
                net.send(k, c, -1, done, ("V", k - 1, lanes[a, k - 1], a, 0))
            events[k, c].append(e)
            now += cost
            if kind == "D":
                for x in sorted(range(len(pairs)), key=lambda x: (x not in ride, x)):
                    if ends(x) == (i, j):
                        ready.add((x, k))
                        if k == 0 < j and x not in high:
                            now = handle(k, c, x, "up", now)
                        if k == n - 1 > i and x not in low:
                            now = handle(k, c, x, "down", now)
            busy[k, c] = now
            return now

        while net.queue:
            now, _, (kind, k, c, a, _) = heapq.heappop(net.queue)
            if kind == "wire":
                net.serve(k, c, now)
                continue
            if kind != "go":
                i, j = ends(a)
                last = k == (j if kind == "U" else i) and a not in ride
                waiting[k, c].append((now + PATIENCE * last, a, kind))
            if busy[k, c] > now + 1e-9:
                continue
            todo = order[k, c]
            more = made[k, c] < len(todo)
            hit = min((
                w for w in waiting[k, c]
                if (w[1], k) in ready and all((d, k) in ready or lanes[d, k] != c for d in ride.get(w[1], ()))
            ), default=None)
            if hit is not None and hit[0] + SLACK * more <= now + 1e-9:
                waiting[k, c].remove(hit)
                net.post(handle(k, c, hit[1], hit[2], now), ("go", k, c, -1, 0))
            elif more:
                made[k, c] += 1
                net.post(handle(k, c, todo[made[k, c] - 1], "D", now), ("go", k, c, -1, 0))
            elif hit is not None:
                net.post(hit[0], ("go", k, c, -1, 0))
        return events, max(busy.values())

    order = {}
    for k in range(n):
        for c in range(cores):
            def rank(a, k=k):
                i, j = ends(a)
                return min(n - 1 - j + k, i + n - 1 - k), any(ends(x) == (i, j) for x in ride), a
            first = [a for a in range(len(pairs)) if all(ends(x) != ends(a) for x in range(a))]
            order[k, c] = sorted((a for a in first if lanes[a, k] == c), key=rank)
    return run(order)


def plans(n, per, half, cores):
    pairs = tile_pairs(n * per, REACH)
    count = len(pairs)
    ride = riders(pairs, n, per, half, cores)
    lanes = lanes_of(pairs, n, per, half, cores, ride)
    own, gather, ends = gather_plan(pairs, n, per, half, cores, lanes, ride)
    scatter, _ = scatter_plan(pairs, n, per, half, cores, lanes, ride, [
        end + EXCHANGE + LAG * (k in (0, n - 1)) for k, end in enumerate(ends)
    ])

    def landings(plan, which):
        uses = {}
        for place, line in plan.items():
            for e in line:
                a = which(e)
                if a is not None:
                    uses.setdefault(a, set()).add(place)
        chosen = colours(uses)
        return chosen, max(chosen.values(), default=-1) + 1

    first_a, size_a = landings(
        gather, lambda e: e["other"] if e["lift"] else e["a"] if e["wait"] and not e["second"] else None
    )
    first_b, size_b = landings(gather, lambda e: e["a"] if e["wait"] and e["second"] and not e["lift"] else None)
    first_u, size_u = landings(scatter, lambda e: e["a"] if e["wait"] and e["u"] else None)
    first_v, size_v = landings(scatter, lambda e: e["a"] if e["wait"] and e["v"] else None)

    def word(a, k, flags):
        p, q = pairs[a]
        code = a | p << 8 | q << 13
        for bit, flag in enumerate(flags):
            code |= int(flag) << (18 + bit)
        if k < n - 1:
            code |= lanes[a, k + 1] << 28
        if k > 0:
            code |= lanes[a, k - 1] << 29
        return code

    def ag_sem(a, twin):
        return size_a + first_b.get(a, 0) if twin else first_a.get(a, 0)

    def rs_sem(a, turned):
        return size_u + first_v.get(a, 0) if turned else first_u.get(a, 0)

    def gather_sems(e):
        waits = ag_sem(e["other"], 0) if e["lift"] else ag_sem(e["a"], e["second"])
        sends = ag_sem(e["a"], 0 if e["cup"] or e["cdn"] or e["fup"] else e["second"])
        return waits | sends << 8 | e["other"] << 16 | e["lower"] << 24 | e["ride"] << 25 | e["lift"] << 26 | e["rest"] << 27

    def scatter_sems(e):
        turned = int(e["dn"] or not e["up"] and e["v"])
        sends = rs_sem(e["other"] if e["side"] else e["a"], turned)
        return rs_sem(e["a"], e["v"]) | sends << 8 | e["other"] << 16 | e["mean"] << 24 | e["second"] << 25

    def pad(lines):
        longest = max(len(line) for line in lines)
        return [line + [(0, 0)] * (longest - len(line)) for line in lines], [len(line) for line in lines]

    places, slots, sends, second, third, ag_sent, rs_sent = [(k, c) for k in range(n) for c in range(cores)], [], [], [], [], [], []
    for k, c in places:
        held = {(row, col): a + count * twin for a, twin, row, col, *_ in own[k, c]}
        slots.append([
            held.get((row, col), 3 * count + row * half + col) for row in range(per) for col in range(half)
        ])
        sends.append([
            (word(a, k, (twin, up, down, side)), ag_sem(a, twin)) for a, twin, _, _, up, down, side in own[k, c]
            if up or down or side
        ])
        second.append([
            (word(e["a"], k, [
                e[f] for f in ("wait", "second", "fup", "fdn", "merge", "cup", "cdn", "comp", "run", "blend")
            ]), gather_sems(e))
            for e in gather[k, c]
        ])
        third.append([
            (word(e["a"], k, [
                e[f] for f in ("comp", "first", "wait", "v", "up", "dn", "fini", "finj", "blend", "side")
            ]), scatter_sems(e))
            for e in scatter[k, c]
        ])
        ag_sent.append(sum(int(up) + int(down) + int(side) for *_, up, down, side in own[k, c])
                       + sum(e["fup"] + e["fdn"] + e["cup"] + e["cdn"] for e in gather[k, c]))
        rs_sent.append(sum(e["up"] + e["dn"] + e["side"] for e in scatter[k, c]))
    return dict(
        count=count, slots=slots, sends=pad(sends), gather=pad(second), scatter=pad(third),
        ag_sent=ag_sent, rs_sent=rs_sent, ag_sems=size_a + size_b, rs_sems=size_u + size_v,
    )


def make_tile_kernel(n, nf, ns, rows, cols, ne, vox_local, n_blocks, regions):
    per = rows // LANES
    half = cols // LANES
    peers = nf * ns
    plan = plans(n, per, half, ns)
    count = plan["count"]
    held = per * half

    def kernel(
        res, green, active_in, aperture, gain, region_in, strength_in, out,
        active, region, strength, sem_small,
        gv, act_col, buf, blocks, rests, img, ar_send, ar_land,
        wgt, dacc, total, powers, size, stage, land,
        sem_g, sem_own, ag_s, ag_r, ar_s, ar_r, rs_s, rs_r,
    ):
        z = lax.axis_index("vox")
        f = lax.axis_index("freq")
        s = lax.axis_index("sub")
        has_up = z < n - 1
        has_down = z > 0
        z_up = jnp.minimum(z + 1, n - 1)
        z_down = jnp.maximum(z - 1, 0)

        def remote(src, dst, send, recv, target):
            return pltpu.make_async_remote_copy(
                src_ref=src, dst_ref=dst, send_sem=send, recv_sem=recv,
                device_id=target, device_id_type=MESH,
            )

        def above(code):
            return {"vox": z_up, "sub": (code >> 28) & 1}

        def below(code):
            return {"vox": z_down, "sub": (code >> 29) & 1}

        def peer(k):
            df, ds = k // ns, k % ns
            return {"freq": lax.rem(f + df, nf), "sub": lax.rem(s + ds, ns)}

        partner = {"sub": lax.rem(s + 1, ns)}

        def has(code, bit):
            return ((code >> (18 + bit)) & 1) == 1

        def lines(t):
            return pl.ds(pl.multiple_of(t * LANES, LANES), LANES)

        role = z * ns + s
        is_role = [role == r for r in range(n * ns)]

        def pick(values):
            usual = max(set(values), key=values.count)
            out_value = jnp.int32(usual)
            for r, value in enumerate(values):
                if value != usual:
                    out_value = jnp.where(is_role[r], jnp.int32(value), out_value)
            return out_value

        def table(lines):
            words, lengths = lines
            columns = [
                [pick([line[e][part] for line in words]) for e in range(len(words[0]))] for part in (0, 1)
            ]

            def at(e):
                found = []
                for level in columns:
                    bit = 0
                    while len(level) > 1:
                        odd = ((e >> bit) & 1) == 1
                        paired = [jnp.where(odd, b, a) for a, b in zip(level[::2], level[1::2])]
                        level, bit = paired + level[len(level) & ~1:], bit + 1
                    found.append(level[0])
                return found

            return at, pick(lengths)

        def drain(sem, sent):
            mine = pick(sent)
            for m in sorted(set(sent)):
                @pl.when(mine == m)
                def _(m=m):
                    block = buf.at[pl.ds(0, m)]
                    remote(block, block, sem, ag_r.at[0], {"vox": z_up}).wait_send()

        barrier = pltpu.get_barrier_semaphore()
        for k in range(1, peers):
            pl.semaphore_signal(barrier, inc=1, device_id=peer(k), device_id_type=MESH)
        for c in range(ns):
            @pl.when(has_up)
            def _():
                pl.semaphore_signal(barrier, inc=1, device_id={"vox": z_up, "sub": c}, device_id_type=MESH)

            @pl.when(has_down)
            def _():
                pl.semaphore_signal(barrier, inc=1, device_id={"vox": z_down, "sub": c}, device_id_type=MESH)

        green_copy = pltpu.make_async_copy(green, gv, sem_g)
        small = [
            pltpu.make_async_copy(a, b, sem_small.at[i])
            for i, (a, b) in enumerate((
                (active_in, active), (region_in, region), (strength_in, strength),
            ))
        ]
        for t in range(held):
            row, col = t // half * LANES, t % half * LANES
            pltpu.make_async_copy(
                res.at[row:row + LANES, col:col + LANES], buf.at[pick([line[t] for line in plan["slots"]])], sem_own
            ).start()
        for c in small:
            c.start()
        green_copy.start()
        own_at, n_own = table(plan["sends"])
        gather_at, n_gather = table(plan["gather"])
        scatter_at, n_scatter = table(plan["scatter"])
        out[...] = jnp.zeros_like(out)
        img[...] = jnp.zeros_like(img)
        blocks[...] = jnp.zeros_like(blocks)
        rests[...] = jnp.zeros_like(rests)
        pl.semaphore_wait(barrier, peers - 1 + ns * has_up.astype(jnp.int32) + ns * has_down.astype(jnp.int32))

        pltpu.make_async_copy(buf.at[pl.ds(0, held)], buf.at[pl.ds(held, held)], sem_own).wait()

        def ag_send(source, target, sem, side):
            remote(buf.at[source], buf.at[target], ag_s, ag_r.at[sem], side).start()

        @pl.loop(0, n_own)
        def _(e):
            code, sem = own_at(e)
            slot = (code & 255) + count * ((code >> 18) & 1)

            @pl.when(has(code, 1))
            def _():
                ag_send(slot, slot, sem, above(code))

            @pl.when(has(code, 2))
            def _():
                ag_send(slot, slot, sem, below(code))

            @pl.when(has(code, 3))
            def _():
                ag_send(slot, slot, sem, partner)

        for c in small:
            c.wait()
        for i in range(ne // LANES):
            line = active[0:1, i * LANES:(i + 1) * LANES].astype(jnp.float32)
            act_col[i * LANES:(i + 1) * LANES, :] = jnp.broadcast_to(line, (LANES, LANES)).T

        def pair_mask(row_tile, col_tile):
            rr = lax.broadcasted_iota(jnp.int32, (LANES, LANES), 0) + row_tile * LANES
            cc = lax.broadcasted_iota(jnp.int32, (LANES, LANES), 1) + col_tile * LANES
            in_band = jnp.abs(rr - cc) <= aperture[0]
            row_on = act_col[lines(row_tile), :] > 0.5
            col_on = active[0:1, lines(col_tile)] > 0
            return in_band & row_on & col_on

        def block_of(p, q):
            return lax.div(p, per) * n + lax.div(q, per)

        def inside(p, q):
            return lines(lax.rem(p, per)), lines(lax.rem(q, per))

        def block_rows(p):
            return pl.ds(pl.multiple_of(lax.div(p, per) * rows, rows), rows)

        def place(p, q):
            value = jnp.where(pair_mask(p, q), total[...], 0.0)
            high = value.astype(jnp.bfloat16)
            rr, cc = inside(p, q)
            blocks[block_of(p, q), rr, cc] = high
            rests[block_of(p, q), rr, cc] = (value - high.astype(jnp.float32)).astype(jnp.bfloat16)

        def image_part(p, q, rest):
            for v in range(vox_local // CHUNK):
                vs = pl.ds(v * CHUNK, CHUNK)
                g = gv[block_rows(q), vs]
                y = jnp.dot(blocks[block_of(p, q)], g, preferred_element_type=jnp.float32)
                if rest:
                    y = y + jnp.dot(rests[block_of(p, q)], g, preferred_element_type=jnp.float32)
                y = y * gv[block_rows(p), vs].astype(jnp.float32)
                img[:, vs] += jnp.sum(y.reshape(rows // 8, 8, CHUNK), axis=0)

        green_copy.wait()
        shape = (LANES, LANES)
        side_of = lax.broadcasted_iota(jnp.int32, shape, 0) - lax.broadcasted_iota(jnp.int32, shape, 1)

        @pl.loop(0, n_gather)
        def _(e):
            code, sems = gather_at(e)
            a, p, q = code & 255, (code >> 8) & 31, (code >> 13) & 31
            slot = a + count * ((code >> 19) & 1)
            merged = a + 2 * count
            other = (sems >> 16) & 255
            lower = (sems >> 24) & 1
            lift = (sems >> 26) & 1
            landed = jnp.where(lift == 1, other, slot)
            sem = (sems >> 8) & 255

            @pl.when(has(code, 0))
            def _():
                remote(buf.at[landed], buf.at[landed], ag_s, ag_r.at[sems & 255], above(code)).wait_recv()

            @pl.when(lift == 1)
            def _():
                both = buf[other].astype(jnp.float32)
                pairs = jnp.where(side_of == 0, both, both + both.T)
                away = side_of * (1 - 2 * lower) > 0
                buf[slot] = jnp.where(away, buf[slot].astype(jnp.float32), pairs).astype(jnp.bfloat16)

            @pl.when(((sems >> 25) & 1) == 1)
            def _():
                kept = side_of * (1 - 2 * lower) <= 0
                buf[a] = jnp.where(kept, buf[other + count * lower].astype(jnp.float32), 0.0).astype(jnp.bfloat16)

            @pl.when(has(code, 2))
            def _():
                ag_send(slot, slot, sem, above(code))

            @pl.when(has(code, 3))
            def _():
                ag_send(slot, slot, sem, below(code))

            @pl.when(has(code, 4))
            def _():
                one = buf[a].astype(jnp.float32)
                two = buf[a + count].astype(jnp.float32).T
                passing = (side_of <= 0) & has(code, 9)
                from_two = side_of * 0 + lower > 0
                both = jnp.where(passing, jnp.where(from_two, two, one), one + two)
                buf[merged] = both.astype(jnp.bfloat16)
                total[...] = both

                @pl.when(has(code, 5))
                def _():
                    ag_send(merged, a, sem, above(code))

                @pl.when(has(code, 6))
                def _():
                    ag_send(merged, a, sem, below(code))

            @pl.when(has(code, 7))
            def _():
                @pl.when(jnp.logical_not(has(code, 4)))
                def _():
                    total[...] = buf[a].astype(jnp.float32)
                place(p, q)

            exact = ((sems >> 27) & 1) == 1

            @pl.when(has(code, 8) & exact)
            def _():
                image_part(p, q, True)

            @pl.when(has(code, 8) & jnp.logical_not(exact))
            def _():
                image_part(p, q, False)

        for b in range(n_blocks):
            ar_send[b:b + 1, :] = jnp.sum(img[:, b * BLOCK:(b + 1) * BLOCK], axis=0, keepdims=True)
        exchanges = [
            remote(ar_send, ar_land.at[k], ar_s.at[k - 1], ar_r.at[k - 1], peer(k)) for k in range(1, peers)
        ]
        for e in exchanges:
            e.start()
        strength_map = jnp.concatenate(
            [jnp.full((1, BLOCK), strength[region[b]], jnp.float32) for b in range(n_blocks)], axis=0
        )

        drain(ag_s, plan["ag_sent"])
        for e in exchanges:
            e.wait_recv()
        image = ar_send[...]
        for k in range(1, peers):
            image = image + ar_land[k]
        scaled = penalize(image, strength_map)
        for b in range(n_blocks):
            img[0:1, b * BLOCK:(b + 1) * BLOCK] = scaled[b:b + 1, :]

        head_row = lax.broadcasted_iota(jnp.int32, (8, LANES), 0)

        def power_of(value):
            largest = jnp.max(jnp.max(jnp.abs(value), axis=0, keepdims=True), axis=1, keepdims=True)
            power = jnp.floor(jnp.log(jnp.maximum(largest, 1e-36)) * (1 / LN2)) + 1.0
            return jnp.broadcast_to(power, (8, LANES))

        def encode(value, power):
            scaled = value * (STEPS * jnp.exp(power * -LN2))
            code = (scaled + jnp.where(scaled >= 0, 0.5, -0.5)).astype(jnp.int32)
            bits = jnp.broadcast_to((power + 128.0).astype(jnp.int32), (8, LANES))
            head = (code[0:8, :] & -2) | ((bits >> head_row) & 1)
            return jnp.concatenate([head, code[8:, :]], axis=0).astype(jnp.int16)

        def decode(slot):
            code = land[slot].astype(jnp.int32)
            bits = jnp.sum(((code[0:8, :] & 1) << head_row).astype(jnp.float32), axis=0, keepdims=True)
            power = bits - 128.0
            return code.astype(jnp.float32) * (jnp.exp(power * LN2) * (1 / STEPS)), power

        def sub_tile(p, q):
            return (block_of(p, q) * per + lax.rem(p, per)) * per + lax.rem(q, per)

        def scatter(slot, sem, target):
            return remote(stage.at[slot], land.at[slot], rs_s, rs_r.at[sem], target)

        @pl.loop(0, n_scatter)
        def _(e):
            code, sems = scatter_at(e)
            a, p, q = code & 255, (code >> 8) & 31, (code >> 13) & 31
            turned = (code >> 21) & 1
            slot = a + count * turned
            other = (sems >> 16) & 255
            wait_sem = sems & 255
            sem = (sems >> 8) & 255

            block = block_of(p, q)
            rr, cc = inside(p, q)

            def weigh(part):
                wgt[part, :] = (gv[part, :].astype(jnp.float32) * img[0:1, :]).astype(jnp.bfloat16)

            @pl.when(has(code, 1))
            def _():
                weigh(block_rows(q))

            @pl.when(((sems >> 25) & 1) == 1)
            def _():
                weigh(block_rows(p))

            def product(left, right):
                return lax.dot_general(left, right, (((1,), (1,)), ((), ())), preferred_element_type=jnp.float32)

            @pl.when(has(code, 0))
            def _():
                dacc[block] = product(gv[block_rows(p), :], wgt[block_rows(q), :])

            @pl.when(((sems >> 24) & 1) == 1)
            def _():
                dacc[block] = 0.5 * (dacc[block] + product(wgt[block_rows(p), :], gv[block_rows(q), :]))

            @pl.when(has(code, 2))
            def _():
                scatter(slot, wait_sem, above(code)).wait_recv()

            @pl.when(has(code, 0))
            def _():
                for x in range(per * per):
                    r0, c0 = x // per * LANES, x % per * LANES
                    powers[block * per * per + x] = power_of(dacc[block, r0:r0 + LANES, c0:c0 + LANES])

            @pl.when(has(code, 4) | has(code, 5))
            def _():
                total[...] = dacc[block, rr, cc]
                size[...] = powers[sub_tile(p, q)]

                @pl.when(has(code, 8))
                def _():
                    d = jnp.where(has(code, 4), q, p)
                    dr, dc = inside(d, d)
                    total[...] = jnp.where(side_of > 0, total[...], dacc[block_of(d, d), dr, dc])
                    size[...] = jnp.maximum(size[...], powers[sub_tile(d, d)])

                @pl.when(has(code, 2))
                def _():
                    value, power = decode(slot)
                    summed = jnp.maximum(size[0:1, :], power) + 1.0
                    stage[slot] = encode(total[...] + value, summed)

                @pl.when(jnp.logical_not(has(code, 2)))
                def _():
                    stage[slot] = encode(total[...], size[0:1, :])

            @pl.when(has(code, 4))
            def _():
                scatter(slot, sem, above(code)).start()

            @pl.when(has(code, 5))
            def _():
                scatter(slot, sem, below(code)).start()

            @pl.when(has(code, 9))
            def _():
                both, power = decode(slot)
                mirrored = jnp.where(side_of <= 0, both, both.T)
                aside = other + count * turned
                stage[aside] = encode(mirrored, power)
                scatter(aside, sem, partner).start()

            @pl.when(has(code, 6) | has(code, 7))
            def _():
                total[...] = dacc[block, rr, cc]

                @pl.when(has_down)
                def _():
                    total[...] += decode(a)[0]

                @pl.when(has_up)
                def _():
                    total[...] += decode(a + count)[0]

            @pl.when(has(code, 6))
            def _():
                new = buf[a].astype(jnp.float32) - gain[0] * total[...]
                out[lines(lax.rem(p, per)), lines(lax.rem(q, half))] = jnp.where(pair_mask(p, q), new, 0.0)

            @pl.when(has(code, 7))
            def _():
                new = buf[a + count].astype(jnp.float32) - gain[0] * total[...].T
                out[lines(lax.rem(q, per)), lines(lax.rem(p, half))] = jnp.where(pair_mask(q, p), new, 0.0)

        for e in exchanges:
            e.wait_send()

        drain(rs_s, plan["rs_sent"])

    dma = pltpu.SemaphoreType.DMA
    tile16 = lambda m: pltpu.VMEM((m, LANES, LANES), jnp.bfloat16)
    scratch = [
        pltpu.VMEM((1, ne), jnp.int32),
        pltpu.SMEM((n_blocks,), jnp.int32),
        pltpu.SMEM((regions,), jnp.float32),
        dma((3,)),
        pltpu.VMEM((ne, vox_local), jnp.bfloat16),
        pltpu.VMEM((ne, LANES), jnp.float32),
        tile16(3 * count + held),
        pltpu.VMEM((n * n, rows, rows), jnp.bfloat16),
        pltpu.VMEM((n * n, rows, rows), jnp.bfloat16),
        pltpu.VMEM((8, vox_local), jnp.float32),
        pltpu.VMEM((n_blocks, BLOCK), jnp.float32),
        pltpu.VMEM((peers, n_blocks, BLOCK), jnp.float32),
        pltpu.VMEM((ne, vox_local), jnp.bfloat16),
        pltpu.VMEM((n * n, rows, rows), jnp.float32),
        pltpu.VMEM((LANES, LANES), jnp.float32),
        pltpu.VMEM((n * n * per * per, 8, LANES), jnp.float32),
        pltpu.VMEM((8, LANES), jnp.float32),
        pltpu.VMEM((2 * count, LANES, LANES), jnp.int16),
        pltpu.VMEM((2 * count, LANES, LANES), jnp.int16),
        dma, dma, dma, dma((plan["ag_sems"],)),
        dma((peers - 1,)), dma((peers - 1,)),
        dma, dma((plan["rs_sems"],)),
    ]
    return kernel, scratch


def make_kernel(n, nf, ns, rows, cols, ne, vox_local, n_blocks, regions):
    tile = min(rows, LANES)
    per = rows // tile
    col_tiles = cols // LANES
    vchunk = min(512, vox_local)
    peers = nf * ns

    def kernel(
        res, green, active_in, aperture_in, gain_in, region_in, strength_in, out,
        active, aperture, gain, region, strength, sem_small,
        allm, gv, act_col, mm, img, ar_send, ar_land, wgt, gacc, flipped, send_buf, land_r, land_l,
        sem_g, sem_own, agr_s, agr_r, agl_s, agl_r, ar_s, ar_r, rsr_s, rsr_r, rsl_s, rsl_r,
    ):
        z = lax.axis_index("vox")
        f = lax.axis_index("freq")
        s = lax.axis_index("sub")
        has_up = z < n - 1
        has_down = z > 0
        up = {"vox": jnp.minimum(z + 1, n - 1)}
        down = {"vox": jnp.maximum(z - 1, 0)}

        def row_of(block):
            return pl.multiple_of(block * rows, rows)

        small = [
            pltpu.make_async_copy(a, b, sem_small.at[i])
            for i, (a, b) in enumerate((
                (active_in, active), (aperture_in, aperture), (gain_in, gain),
                (region_in, region), (strength_in, strength),
            ))
        ]
        for c in small:
            c.start()
        own_copy = pltpu.make_async_copy(res, allm.at[pl.ds(row_of(z), rows), :], sem_own)
        own_copy.start()
        green_copy = pltpu.make_async_copy(green, gv, sem_g)
        green_copy.start()

        def peer(k):
            df, ds = k // ns, k % ns
            return {"freq": lax.rem(f + df, nf), "sub": lax.rem(s + ds, ns)}

        barrier = pltpu.get_barrier_semaphore()
        for k in range(1, peers):
            pl.semaphore_signal(barrier, inc=1, device_id=peer(k), device_id_type=MESH)

        @pl.when(has_up)
        def _():
            pl.semaphore_signal(barrier, inc=1, device_id=up, device_id_type=MESH)

        @pl.when(has_down)
        def _():
            pl.semaphore_signal(barrier, inc=1, device_id=down, device_id_type=MESH)

        pl.semaphore_wait(barrier, peers - 1 + has_up.astype(jnp.int32) + has_down.astype(jnp.int32))

        def square(q):
            local = q * tile - s * cols
            inside = (local >= 0) & (local < cols)
            return inside, lax.div(jnp.clip(local, 0, cols - 1), LANES)

        def band(q, kind):
            reach = q * tile - s * cols + ne
            shift = ne // LANES + APERTURE_MAX // LANES + 1
            lift = LANES * (shift - ne // LANES)
            first = lax.div(reach + lift - APERTURE_MAX, LANES) - shift
            last = lax.div(reach + lift + tile - 1 + APERTURE_MAX, LANES) - shift + 1
            first = jnp.clip(first, 0, col_tiles)
            last = jnp.clip(last, 0, col_tiles)
            if kind != FULL:
                inside, diag = square(q)
            if kind == UP:
                last = jnp.where(inside, jnp.minimum(last, diag + 1), last)
            if kind == DOWN:
                first = jnp.where(inside, jnp.maximum(first, diag), first)
            return first, last - first

        def per_width(q, fn, kind=FULL):
            first, count = band(q, kind)
            for w in range(1, col_tiles + 1):
                @pl.when(count == w)
                def _(w=w):
                    fn(pl.ds(pl.multiple_of(first * LANES, LANES), w * LANES))

        def tile_rows(q):
            return pl.ds(pl.multiple_of(q * tile, tile), tile)

        def remote(src, dst, send, recv, target):
            return pltpu.make_async_remote_copy(
                src_ref=src, dst_ref=dst, send_sem=send, recv_sem=recv,
                device_id=target, device_id_type=MESH,
            )

        def each_tile(block, make, act, kind=FULL):
            for t in range(per):
                q = block * per + t
                per_width(q, lambda c, q=q: act(make(q, c)), kind)

        def gather_up(q, c):
            a = allm.at[tile_rows(q), c]
            return remote(a, a, agr_s.at[q], agr_r.at[q], up)

        def gather_down(q, c):
            a = allm.at[tile_rows(q), c]
            return remote(a, a, agl_s.at[q], agl_r.at[q], down)

        for t in range(per):
            q = z * per + t

            def first_up(c, q=q, t=t):
                remote(res.at[pl.ds(t * tile, tile), c], allm.at[tile_rows(q), c],
                       agr_s.at[q], agr_r.at[q], up).start()

            def first_down(c, q=q, t=t):
                remote(res.at[pl.ds(t * tile, tile), c], allm.at[tile_rows(q), c],
                       agl_s.at[q], agl_r.at[q], down).start()

            @pl.when(has_up)
            def _():
                per_width(q, first_up)

            @pl.when(has_down)
            def _():
                per_width(q, first_down)

        for c in small:
            c.wait()
        for i in range(ne // LANES):
            line = active[0:1, i * LANES:(i + 1) * LANES].astype(jnp.float32)
            act_col[i * LANES:(i + 1) * LANES, :] = jnp.broadcast_to(line, (LANES, LANES)).T
        img[...] = jnp.zeros_like(img)
        col0 = pl.multiple_of(s * cols, cols)

        def pair_mask(block):
            r0 = row_of(block)
            rr = lax.broadcasted_iota(jnp.int32, (rows, cols), 0) + r0
            cc = lax.broadcasted_iota(jnp.int32, (rows, cols), 1) + col0
            in_band = jnp.abs(rr - cc) <= aperture[0]
            row_on = act_col[pl.ds(r0, rows), 0:1] > 0.5
            col_on = active[0:1, pl.ds(col0, cols)] > 0
            return in_band & row_on & col_on

        def image_part(block):
            r0 = row_of(block)
            value = allm[pl.ds(r0, rows), :].astype(jnp.float32)
            mm[...] = jnp.where(pair_mask(block), value, 0.0).astype(jnp.bfloat16)

            @pl.loop(0, vox_local // vchunk)
            def _(v):
                vs = pl.ds(pl.multiple_of(v * vchunk, vchunk), vchunk)
                y = jnp.dot(mm[...], gv[pl.ds(col0, cols), vs], preferred_element_type=jnp.float32)
                y = y * gv[pl.ds(r0, rows), vs].astype(jnp.float32)
                img[:, vs] += jnp.sum(y.reshape(rows // 8, 8, vchunk), axis=0)

        own_copy.wait()
        green_copy.wait()
        image_part(z)

        @pl.loop(0, n - 1)
        def _(step):
            from_below = z - 1 - step
            from_above = z + 1 + step
            for t in range(per):
                @pl.when(from_below >= 0)
                def _():
                    q = from_below * per + t

                    def land(c):
                        gather_up(q, c).wait_recv()

                        @pl.when(has_up)
                        def _():
                            gather_up(q, c).start()
                    per_width(q, land)

                @pl.when(from_above < n)
                def _():
                    q = from_above * per + t

                    def land(c):
                        gather_down(q, c).wait_recv()

                        @pl.when(has_down)
                        def _():
                            gather_down(q, c).start()
                    per_width(q, land)

            @pl.when(from_below >= 0)
            def _():
                image_part(from_below)

            @pl.when(from_above < n)
            def _():
                image_part(from_above)

        ar_send[...] = jnp.sum(img[...], axis=0, keepdims=True)
        exchanges = [
            remote(ar_send, ar_land.at[k], ar_s.at[k], ar_r.at[k], peer(k)) for k in range(1, peers)
        ]
        for e in exchanges:
            e.start()
        strength_map = jnp.concatenate(
            [jnp.full((1, BLOCK), strength[region[b]], jnp.float32) for b in range(n_blocks)], axis=1
        )

        @pl.loop(0, n)
        def _(b):
            @pl.when(has_up & (b <= z))
            def _():
                each_tile(b, gather_up, lambda c: c.wait_send())

            @pl.when(has_down & (b >= z))
            def _():
                each_tile(b, gather_down, lambda c: c.wait_send())

        for e in exchanges:
            e.wait_recv()
        total = ar_send[...]
        for k in range(1, peers):
            total = total + ar_land[k]
        img[0:1, :] = penalize(total, strength_map)

        wrows = 32

        @pl.loop(0, cols // wrows)
        def _(i):
            src = pl.ds(pl.multiple_of(col0 + i * wrows, wrows), wrows)
            dst = pl.ds(pl.multiple_of(i * wrows, wrows), wrows)
            wgt[dst, :] = (gv[src, :].astype(jnp.float32) * img[0:1, :]).astype(jnp.bfloat16)

        def scatter_up(q, c):
            return remote(send_buf.at[tile_rows(q), c], land_r.at[tile_rows(q), c],
                          rsr_s.at[q], rsr_r.at[q], up)

        def scatter_down(q, c):
            return remote(send_buf.at[tile_rows(q), c], land_l.at[tile_rows(q), c],
                          rsl_s.at[q], rsl_r.at[q], down)

        def partial_step(k, ends):
            lo, hi = ends
            use_hi = (hi > z) & ((lo >= z) | (z + (n - 1 - hi) <= (n - 1 - z) + lo))
            d = jnp.where(use_hi, hi, lo)
            rs = pl.ds(row_of(d), rows)
            part = lax.dot_general(
                gv[rs, :], wgt[...], (((1,), (1,)), ((), ())), preferred_element_type=jnp.float32
            )
            gacc[rs, :] = part
            sends_up = (d > z) & jnp.logical_not(has_down)
            sends_down = (d < z) & jnp.logical_not(has_up)

            @pl.when(sends_up | sends_down)
            def _():
                send_buf[rs, :] = part.astype(jnp.bfloat16)

            @pl.when(sends_up)
            def _():
                each_tile(d, scatter_up, lambda c: c.start(), UP)

            @pl.when(sends_down)
            def _():
                each_tile(d, scatter_down, lambda c: c.start(), DOWN)

            step_hi = use_hi.astype(jnp.int32)
            return lo + 1 - step_hi, hi - step_hi

        lax.fori_loop(0, n, partial_step, (jnp.int32(0), jnp.int32(n - 1)))

        @pl.loop(0, n - 1)
        def _(slot):
            @pl.when(has_down & (slot >= z))
            def _():
                d = z + n - 1 - slot
                for t in range(per):
                    q = d * per + t

                    def add(c):
                        scatter_up(q, c).wait_recv()
                        send_buf[tile_rows(q), c] = (
                            gacc[tile_rows(q), c] + land_r[tile_rows(q), c].astype(jnp.float32)
                        ).astype(jnp.bfloat16)
                        scatter_up(q, c).start()
                    per_width(q, add, UP)

            @pl.when(has_up & (slot >= n - 1 - z))
            def _():
                d = slot - (n - 1 - z)
                for t in range(per):
                    q = d * per + t

                    def add(c):
                        scatter_down(q, c).wait_recv()
                        send_buf[tile_rows(q), c] = (
                            gacc[tile_rows(q), c] + land_l[tile_rows(q), c].astype(jnp.float32)
                        ).astype(jnp.bfloat16)
                        scatter_down(q, c).start()
                    per_width(q, add, DOWN)

        @pl.when(has_down)
        def _():
            each_tile(z, scatter_up, lambda c: c.wait_recv(), UP)

        @pl.when(has_up)
        def _():
            each_tile(z, scatter_down, lambda c: c.wait_recv(), DOWN)

        mine = pl.ds(row_of(z), rows)
        def add_landed(land, there, q, mirrored):
            inside, diag = square(q)
            offset = lax.rem(q * tile, LANES)
            for j in range(col_tiles):
                c = slice(j * LANES, (j + 1) * LANES)
                flip = inside & mirrored(j, diag)

                @pl.when(there & jnp.logical_not(flip))
                def _():
                    gacc[tile_rows(q), c] += land[tile_rows(q), c].astype(jnp.float32)

                @pl.when(there & flip)
                def _():
                    twin = pl.ds(pl.multiple_of(col0 + j * LANES, LANES), LANES)
                    own = pl.ds(pl.multiple_of(diag * LANES, LANES), LANES)
                    flipped[...] = land[twin, own].astype(jnp.float32).T
                    gacc[tile_rows(q), c] += flipped[pl.ds(pl.multiple_of(offset, tile), tile), :]

        for t in range(per):
            add_landed(land_r, has_down, z * per + t, lambda j, diag: j > diag)
            add_landed(land_l, has_up, z * per + t, lambda j, diag: j < diag)
        gradient = gacc[mine, :]
        data = allm[mine, :].astype(jnp.float32)
        out[...] = jnp.where(pair_mask(z), data - gain[0] * gradient, 0.0)

        for e in exchanges:
            e.wait_send()

        @pl.loop(0, n)
        def _(b):
            @pl.when(has_up & (b > z))
            def _():
                each_tile(b, scatter_up, lambda c: c.wait_send(), UP)

            @pl.when(has_down & (b < z))
            def _():
                each_tile(b, scatter_down, lambda c: c.wait_send(), DOWN)

    tiles = n * per
    dma = pltpu.SemaphoreType.DMA
    scratch = [
        pltpu.VMEM((1, ne), jnp.int32),
        pltpu.SMEM((1,), jnp.int32),
        pltpu.SMEM((1,), jnp.float32),
        pltpu.SMEM((n_blocks,), jnp.int32),
        pltpu.SMEM((regions,), jnp.float32),
        dma((5,)),
        pltpu.VMEM((ne, cols), jnp.bfloat16),
        pltpu.VMEM((ne, vox_local), jnp.bfloat16),
        pltpu.VMEM((ne, LANES), jnp.float32),
        pltpu.VMEM((rows, cols), jnp.bfloat16),
        pltpu.VMEM((8, vox_local), jnp.float32),
        pltpu.VMEM((1, vox_local), jnp.float32),
        pltpu.VMEM((peers, 1, vox_local), jnp.float32),
        pltpu.VMEM((cols, vox_local), jnp.bfloat16),
        pltpu.VMEM((ne, cols), jnp.float32),
        pltpu.VMEM((LANES, LANES), jnp.float32),
        pltpu.VMEM((ne, cols), jnp.bfloat16),
        pltpu.VMEM((ne, cols), jnp.bfloat16),
        pltpu.VMEM((ne, cols), jnp.bfloat16),
        dma, dma,
        dma((tiles,)), dma((tiles,)), dma((tiles,)), dma((tiles,)),
        dma((peers,)), dma((peers,)),
        dma((tiles,)), dma((tiles,)), dma((tiles,)), dma((tiles,)),
    ]
    return kernel, scratch


def tiled(sizes, rows, cols, ne, vox_local):
    n, ns = sizes["vox"], sizes["sub"]
    return (
        rows % LANES == 0 and vox_local % CHUNK == 0 and rows * n == ne and cols * ns == ne
        and n > 1 and ns > 1 and cols % rows == 0 and ne // LANES <= 32
        and len(tile_pairs(ne // LANES, REACH)) <= 256
    )


def solution(mesh):
    sizes = dict(mesh.shape)

    def body(residual, green, active, aperture, step_gain, block_region, strength):
        _, rows, cols = residual.shape
        _, ne, vox_local = green.shape
        tiles = tiled(sizes, rows, cols, ne, vox_local)
        make = make_tile_kernel if tiles else make_kernel
        kernel, scratch = make(
            sizes["vox"], sizes["freq"], sizes["sub"], rows, cols, ne, vox_local,
            block_region.shape[0], strength.shape[0],
        )
        vmem = pl.BlockSpec(memory_space=pltpu.VMEM)
        hbm = pl.BlockSpec(memory_space=pltpu.HBM)
        updated = pl.pallas_call(
            kernel,
            out_shape=jax.ShapeDtypeStruct((rows, cols), jnp.float32),
            in_specs=[hbm] * 3 + [pl.BlockSpec(memory_space=pltpu.SMEM) if tiles else hbm] * 2 + [hbm] * 2,
            out_specs=vmem,
            scratch_shapes=scratch,
            compiler_params=pltpu.CompilerParams(
                collective_id=0, has_side_effects=True, vmem_limit_bytes=32 * 1024 * 1024
            ),
            name="imaging_step",
        )(*[
            pltpu.with_memory_space_constraint(a, pltpu.HBM) if a.size > 1 else a
            for a in (residual[0], green[0], active, aperture, step_gain, block_region, strength)
        ])
        return updated[None]

    in_specs = (
        P(("groups", "freq"), "vox", "sub"),
        P(("groups", "freq"), None, "vox"),
        P(("groups", "freq"), None),
        P(("groups", "freq")),
        P(("groups", "freq")),
        P(("groups", "vox")),
        P(),
    )
    out_specs = P(("groups", "freq"), "vox", "sub")
    return jax.shard_map(body, mesh=mesh, in_specs=in_specs, out_specs=out_specs, check_vma=False)
```
